512 devices in a mesh: plane: 32 (over x, z), tile: 16 (over y, core).
Axes of the slice: x: 4, y: 8, z: 8, core: 2. Of those that a mesh axis runs over, the one named last changes fastest.
Arguments:
- raw_planes: bfloat16 [3072, 512, 512], P('plane', 'tile'), may hold values from -6 to 6
- pair_sections: int32 [2048, 2], P('plane'), may hold values from 0 to 47
- pair_rows: int32 [2048, 2], P('plane'), may hold values from 0 to 128
- pair_extent: int32 [2048], P('plane'), may hold values from 64 to 128
- pair_owner: int32 [2048, 1], P('plane'), may hold values from 0 to 15; in each aligned block of 64 rows (0 to 63, 64 to 127, ...) at most 12 rows name the same one
Outputs:
- surface_out: bfloat16 [6144, 128, 256], P(('plane', 'tile'))
The draws below stay inside these ranges and needn't reach their ends.
Inputs may be any that keep to these rules, and one draw needn't show every extreme that they name: `pair_owner`: among the 64 pairs of one slab no owner takes more than 12 pairs.
All inputs are finite; a program needn't handle non-finite values.
Results may differ from the reference program's by a relative error of at most 0.012.
The reference program's roundings to bfloat16 on the way count: a program that leaves them out, or rounds other values in their place, can miss the bound.
Values may be sent and summed in bfloat16 or wider, within the bound.
No kernel may reach another device: no remote copies, remote signals or barrier semaphores. Data moves between devices by JAX's collectives and lax.ppermute only.
A program may use at most 64 MiB of HBM per device.

```python
import math
import jax
import jax.numpy as jnp
import numpy as np
from jax import lax

HALF = 256
FACE = 512
BAND = 128
SEC = 3
NZ = 3072
OWN_CAP = 12
PAIRS_G = 64
PAIRS = 2048
N_PLANE = 32
N_TILE = 16


def set_ends(drawn, own_key, low, high):
    longest = drawn.shape.index(max(drawn.shape))
    spots = []
    for shift in (0, 1):
        where = [jax.random.randint(jax.random.fold_in(own_key, axis), (), 0, length) for axis, length in enumerate(drawn.shape)]
        where[longest] = (where[longest] + shift) % drawn.shape[longest]
        spots.append(tuple(where))
    return drawn.at[spots[0]].set(low).at[spots[1]].set(high)


def level_of(rng, shape, split, low, top_value):
    loudness = 1.0
    for axis_at, parts in split:
        draws = jax.random.uniform(jax.random.fold_in(jax.random.fold_in(rng, 6), axis_at), (parts,), jnp.float32, low / len(split), top_value / len(split))
        loudness = loudness * jnp.repeat(jnp.exp(draws), shape[axis_at] // parts).reshape((-1,) + (1,) * (len(shape) - 1 - axis_at))
    return loudness


def deal_out(key, own, number, rows, number_of, top, bound, slope):
    ranking = jax.random.permutation(key, number_of)
    heavy_load, ordinary = load_shares(number_of, rows * top, bound, slope, True), load_shares(number_of, rows * top, bound, slope, False)
    places = jnp.arange(number_of)

    def named(lengths, rotation):
        used = int((lengths > 0).sum())
        fixed = max(1, used // 4)
        moved = fixed + (places - fixed + rotation * (used - fixed)) % max(1, number_of - fixed)
        return jnp.zeros((number_of,), jnp.int32).at[ranking[jnp.where(places < fixed, places, moved)]].set(jnp.asarray(lengths, jnp.int32))

    lengths = jnp.where(number % 4 == 0, named(heavy_load, number // 4), named(ordinary, number - number // 4 - 1))
    mixed = jax.random.permutation(jax.random.fold_in(own, 3), number_of)
    giver, sink = mixed[0:number_of // 2 * 2:2], mixed[1:number_of // 2 * 2:2]
    room = jnp.minimum(lengths[giver] - 1, bound - lengths[sink]) // 2
    room = jnp.where((giver == ranking[0]) | (sink == ranking[0]) | (lengths[sink] == 0), 0, jnp.maximum(room, 0))
    moved = jax.random.randint(jax.random.fold_in(own, 4), (number_of // 2,), 0, 1 << 20) % (room + 1)
    lengths = lengths.at[giver].add(-moved).at[sink].add(moved)
    members = jnp.searchsorted(jnp.cumsum(lengths), jnp.arange(rows * top), side="right").astype(jnp.int32)
    grid = members.reshape(top, rows).T
    grid = grid[jax.random.permutation(jax.random.fold_in(own, 1), rows)]
    rotation = jax.random.randint(jax.random.fold_in(own, 2), (rows, 1), 0, top)
    return jnp.take_along_axis(grid, (jnp.arange(top)[None, :] + rotation) % top, axis=1)


def load_shares(count, total, bound, skew, full):
    loads = [(1 << 20) // math.isqrt(grade ** skew) + 1 for grade in range(1, count + 1)]
    largest = bound if full else min(bound, max(-(-total // count), total * loads[0] // sum(loads)))
    least = 1 if total - largest >= count - 1 else 0
    counts, rest = [largest] + [least] * (count - 1), total - largest - least * (count - 1)
    while rest > 0:
        free = [i for i in range(1, count) if counts[i] < largest] or [i for i in range(1, count) if counts[i] < bound]
        mass, remaining = sum([loads[i] for i in free]), rest
        for i in free:
            addition = min(bound - counts[i], max(1, remaining * loads[i] // mass), rest)
            counts[i] = counts[i] + addition
            rest = rest - addition
    return np.array(counts)


def centred(own_key, shape, spread, most, split=(), held_as=jnp.bfloat16):
    result = spread * jax.random.normal(own_key, shape, jnp.float32)
    if split:
        result = result * level_of(own_key, shape, split, -0.22, 0.18)
    return jnp.clip(result, -most, most).astype(held_as)


def setup_inputs(seed: int = 0) -> dict:
    seeds = jax.random.split(jax.random.key(seed), 6)
    raw_planes = centred(seeds[0], (NZ, FACE, FACE), 1.0, 6.0, ((0, 32), (1, 16)))
    pair_sections = set_ends(jax.random.randint(seeds[1], (PAIRS, 2), 0, SEC * N_TILE), jax.random.fold_in(seeds[1], 1), 0, (SEC * N_TILE) - 1).astype(jnp.int32)
    pair_rows = set_ends(jax.random.randint(seeds[2], (PAIRS, 2), 0, HALF - BAND + 1), jax.random.fold_in(seeds[2], 1), 0, HALF - BAND).astype(jnp.int32)
    pair_extent = set_ends(jax.random.randint(seeds[3], (PAIRS,), BAND // 2, BAND + 1), jax.random.fold_in(seeds[3], 1), BAND // 2, BAND).astype(jnp.int32)
    pair_owner_keys = jax.random.split(jax.random.fold_in(seeds[4], 1), PAIRS // PAIRS_G)
    pair_owner_turns = jax.random.permutation(jax.random.fold_in(seeds[4], 3), PAIRS // PAIRS_G)
    pair_owner = jax.vmap(lambda own, number: deal_out(jax.random.fold_in(seeds[4], 2), own, number, PAIRS_G, N_TILE, 1, OWN_CAP, 2))(pair_owner_keys, pair_owner_turns).reshape((PAIRS, 1))
    return {"raw_planes": raw_planes, "pair_sections": pair_sections, "pair_rows": pair_rows, "pair_extent": pair_extent, "pair_owner": pair_owner}


def blur_matrix(face_cells, half_cells):
    source = jnp.arange(face_cells, dtype=jnp.int32)[:, None]
    target = jnp.arange(half_cells, dtype=jnp.int32)[None, :]
    offset = jnp.abs(source - 2 * target)
    weights = jnp.where(offset == 0, 6.0, jnp.where(offset == 1, 4.0, jnp.where(offset == 2, 1.0, 0.0)))
    return (weights * 0.0625).astype(jnp.bfloat16)

def dft_tables(length):
    indices = jnp.arange(length, dtype=jnp.int32)
    phases = indices[:, None] * indices[None, :] % length
    angles = phases.astype(jnp.float32) * (2.0 * math.pi / length)
    factor = 1.0 / math.sqrt(length)
    return ((jnp.cos(angles) * factor).astype(jnp.bfloat16), (jnp.sin(angles) * factor).astype(jnp.bfloat16))

def spectrum(band_cells, cos_half, sin_half, cos_band, sin_band):
    row_real = jnp.dot(band_cells, cos_half, preferred_element_type=jnp.float32).astype(jnp.bfloat16)
    row_imag = (-jnp.dot(band_cells, sin_half, preferred_element_type=jnp.float32)).astype(jnp.bfloat16)
    spec_real = jnp.dot(cos_band, row_real, preferred_element_type=jnp.float32) + jnp.dot(sin_band, row_imag, preferred_element_type=jnp.float32)
    spec_imag = jnp.dot(cos_band, row_imag, preferred_element_type=jnp.float32) - jnp.dot(sin_band, row_real, preferred_element_type=jnp.float32)
    return (spec_real, spec_imag)

def correlate_pair(first_band, second_band, cos_half, sin_half, cos_band, sin_band):
    first_real, first_imag = spectrum(first_band, cos_half, sin_half, cos_band, sin_band)
    second_real, second_imag = spectrum(second_band, cos_half, sin_half, cos_band, sin_band)
    cross_real = first_real * second_real + first_imag * second_imag
    cross_imag = first_imag * second_real - first_real * second_imag
    magnitude = jnp.sqrt(cross_real * cross_real + cross_imag * cross_imag)
    mean_level = jnp.mean(magnitude) + 1e-06
    divisor = magnitude + mean_level
    norm_real = (cross_real / divisor).astype(jnp.bfloat16)
    norm_imag = (cross_imag / divisor).astype(jnp.bfloat16)
    col_real = (jnp.dot(cos_band, norm_real, preferred_element_type=jnp.float32) - jnp.dot(sin_band, norm_imag, preferred_element_type=jnp.float32)).astype(jnp.bfloat16)
    col_imag = (jnp.dot(cos_band, norm_imag, preferred_element_type=jnp.float32) + jnp.dot(sin_band, norm_real, preferred_element_type=jnp.float32)).astype(jnp.bfloat16)
    surface = jnp.dot(col_real, cos_half, preferred_element_type=jnp.float32) - jnp.dot(col_imag, sin_half, preferred_element_type=jnp.float32)
    return surface.astype(jnp.bfloat16)

def reference(raw_planes, pair_sections, pair_rows, pair_extent, pair_owner):
    blur_table = blur_matrix(FACE, HALF)

    def reduce_plane(plane_cells):
        across = jnp.dot(plane_cells, blur_table, preferred_element_type=jnp.float32).astype(jnp.bfloat16)
        return jnp.dot(blur_table.T, across, preferred_element_type=jnp.float32).astype(jnp.bfloat16)
    planar = lax.map(reduce_plane, raw_planes)
    previous = jnp.concatenate([jnp.zeros((1, HALF, HALF), planar.dtype), planar[:-1]], axis=0)
    sections = ((previous[0::2].astype(jnp.float32) + 2.0 * planar[0::2].astype(jnp.float32) + planar[1::2].astype(jnp.float32)) * 0.25).astype(jnp.bfloat16)
    cos_half, sin_half = dft_tables(HALF)
    cos_band, sin_band = dft_tables(BAND)
    group_size = SEC * N_TILE
    pair_index = jnp.arange(PAIRS, dtype=jnp.int32)
    group_of = pair_index // PAIRS_G
    first_ids = (group_of * group_size + pair_sections[:, 0]).astype(jnp.int32)
    second_ids = (group_of * group_size + pair_sections[:, 1]).astype(jnp.int32)
    row_index = jnp.arange(BAND, dtype=jnp.int32)
    zero_index = jnp.zeros((), jnp.int32)

    def one_pair(packed):
        first_id, second_id, first_row, second_row, extent = packed
        live_rows = (row_index < extent)[:, None]
        first_band = lax.dynamic_slice(sections, (first_id.astype(jnp.int32), first_row.astype(jnp.int32), zero_index), (1, BAND, HALF))[0]
        second_band = lax.dynamic_slice(sections, (second_id.astype(jnp.int32), second_row.astype(jnp.int32), zero_index), (1, BAND, HALF))[0]
        first_band = jnp.where(live_rows, first_band, jnp.zeros_like(first_band))
        second_band = jnp.where(live_rows, second_band, jnp.zeros_like(second_band))
        return correlate_pair(first_band, second_band, cos_half, sin_half, cos_band, sin_band)
    surfaces = lax.map(one_pair, (first_ids, second_ids, pair_rows[:, 0], pair_rows[:, 1], pair_extent))
    owners = pair_owner[:, 0].reshape(N_PLANE, PAIRS_G)
    position = jnp.arange(PAIRS_G, dtype=jnp.int32)
    earlier = (owners[:, :, None] == owners[:, None, :]) & (position[None, None, :] < position[None, :, None])
    slot_of = lax.optimization_barrier(jnp.sum(earlier.astype(jnp.int32), axis=2))
    groups = jnp.arange(N_PLANE, dtype=jnp.int32)[:, None]
    destination = ((groups * N_TILE + owners) * OWN_CAP + slot_of).reshape(PAIRS)
    surface_out = jnp.zeros((N_PLANE * N_TILE * OWN_CAP, BAND, HALF), jnp.bfloat16)
    return surface_out.at[destination].set(surfaces)
```

```python
import functools
import math

import jax
import jax.numpy as jnp
import numpy as np
from jax import lax
from jax.experimental import pallas as pl
from jax.experimental.pallas import tpu as pltpu
from jax.sharding import PartitionSpec as P

BAND = 128
OWN_CAP = 12
FACE = 512
HALF = 256
TILES = 16
FREQS = 8
GROUP = 8
VMEM_LIMIT = 24 * 1024 * 1024


def whole(space=pltpu.VMEM):
    return pl.BlockSpec(memory_space=space)


def params(**kw):
    return pltpu.CompilerParams(vmem_limit_bytes=VMEM_LIMIT, **kw)


def blur_weight(offset):
    offset = abs(offset)
    return (6.0, 4.0, 1.0)[offset] / 16.0 if offset <= 2 else 0.0


def blur_matrix():
    table = np.zeros((FACE, HALF), np.float32)
    for c in range(FACE):
        for j in range(HALF):
            if abs(c - 2 * j) <= 2:
                table[c, j] = blur_weight(c - 2 * j)
    return table.astype(jnp.bfloat16)


def dft_tables(length):
    indices = np.arange(length)
    phases = indices[:, None] * indices[None, :] % length
    angles = phases.astype(np.float32) * np.float32(2.0 * math.pi / length)
    factor = np.float32(1.0 / math.sqrt(length))
    return (
        (np.cos(angles) * factor).astype(jnp.bfloat16),
        (np.sin(angles) * factor).astype(jnp.bfloat16),
    )


def halo_select():
    table = np.zeros((GROUP * 4, GROUP * 32), np.float32)
    for q in range(GROUP):
        for h in range(4):
            table[q * 4 + h, q * 32 + 28 + h] = 1.0
    return table.astype(jnp.bfloat16)


def column_weights(first_tile):
    local = np.zeros((16, 32), np.float32)
    halo = np.zeros((16, 4), np.float32)
    for i in range(16):
        for c in range(32):
            local[i, c] = blur_weight(c + 2 - 2 * i)
        for h in range(4):
            halo[i, h] = blur_weight(h - 2 - 2 * i)
    if first_tile:
        local[0, 0] = 0.0
        halo[1, :] = 0.0
    return local, halo


def column_tables():
    grouped = np.zeros((2, GROUP * 16, GROUP * 36), np.float32)
    single = np.zeros((2, 16, 64), np.float32)
    for variant in (0, 1):
        local, halo = column_weights(variant == 0)
        for q in range(GROUP):
            rows = slice(q * 16, q * 16 + 16)
            grouped[variant, rows, q * 32 : q * 32 + 32] = local
            at = GROUP * 32 + q * 4
            grouped[variant, rows, at : at + 4] = halo
        single[variant, :, :32] = local
        single[variant, :, 60:64] = halo
    return grouped.astype(jnp.bfloat16), single.astype(jnp.bfloat16)


def row_transform_table():
    cos_half, sin_half = dft_tables(HALF)
    table = np.zeros((HALF, HALF), np.float32)
    for d in range(TILES):
        for f in range(FREQS):
            v = d * FREQS + f
            table[d * 16 + f] = cos_half[v]
            if v:
                table[d * 16 + FREQS + f] = -sin_half[v].astype(np.float32)
            else:
                table[d * 16 + FREQS + f] = cos_half[HALF // 2]
    return table.astype(jnp.bfloat16)


def row_inverse_table():
    cos_half, sin_half = dft_tables(HALF)
    table = np.zeros((HALF, HALF), np.float32)
    for v in range(HALF // 2):
        table[v] = cos_half[v].astype(np.float32) * (2.0 if v else 1.0)
        if v:
            table[HALF // 2 + v] = sin_half[v].astype(np.float32) * -2.0
        else:
            table[HALF // 2] = cos_half[HALF // 2]
    return table.astype(jnp.bfloat16)


def reversal():
    table = np.zeros((BAND, BAND), np.float32)
    for u in range(BAND):
        table[(BAND - u) % BAND, u] = 1.0
    return table.astype(jnp.bfloat16)


def dot(a, b):
    return jnp.dot(a, b, preferred_element_type=jnp.float32)


def dot_nt(a, b):
    return lax.dot_general(
        a, b, (((1,), (1,)), ((), ())), preferred_element_type=jnp.float32
    )


def across_kernel(raw_ref, table_ref, select_ref, across_ref, edge_ref):
    for k in range(raw_ref.shape[0] // GROUP):
        cells = raw_ref[k * GROUP : (k + 1) * GROUP].reshape(GROUP * 32, FACE)
        across = dot(cells, table_ref[...]).astype(jnp.bfloat16)
        across_ref[k] = across
        edge_ref[k] = dot(select_ref[...], across).astype(jnp.bfloat16)


def blur_across(raw, table, select):
    planes = raw.shape[0]
    groups = planes // GROUP
    step = 2
    return pl.pallas_call(
        across_kernel,
        grid=(groups // step,),
        in_specs=[
            pl.BlockSpec((step * GROUP, 32, FACE), lambda g: (g, 0, 0)),
            pl.BlockSpec((FACE, HALF), lambda g: (0, 0)),
            pl.BlockSpec((GROUP * 4, GROUP * 32), lambda g: (0, 0)),
        ],
        out_specs=[
            pl.BlockSpec((step, GROUP * 32, HALF), lambda g: (g, 0, 0)),
            pl.BlockSpec((step, GROUP * 4, HALF), lambda g: (g, 0, 0)),
        ],
        out_shape=[
            jax.ShapeDtypeStruct((groups, GROUP * 32, HALF), jnp.bfloat16),
            jax.ShapeDtypeStruct((groups + 1, GROUP * 4, HALF), jnp.bfloat16),
        ],
        compiler_params=params(),
        cost_estimate=pl.CostEstimate(
            flops=2 * planes * 32 * FACE * HALF,
            bytes_accessed=planes * 32 * (FACE + HALF) * 2,
            transcendentals=0,
        ),
        name="blur_across",
    )(raw, table, select)


def behind_kernel(plane_ref, table_ref, edges_in_ref, edge_ref):
    edge_ref[0] = dot(plane_ref[...], table_ref[...]).astype(jnp.bfloat16)


def blur_behind(plane, table, edges):
    last = edges.shape[0] - 1
    return pl.pallas_call(
        behind_kernel,
        grid=(1,),
        in_specs=[
            pl.BlockSpec((32, FACE), lambda g: (0, 0)),
            pl.BlockSpec((FACE, HALF), lambda g: (0, 0)),
            pl.BlockSpec(memory_space=pl.ANY),
        ],
        out_specs=pl.BlockSpec((1, 32, HALF), lambda g: (last, 0, 0)),
        out_shape=jax.ShapeDtypeStruct(edges.shape, jnp.bfloat16),
        input_output_aliases={2: 0},
        compiler_params=params(),
        name="blur_behind",
    )(plane, table, edges)


def section_kernel(
    tile_ref, first_ref, across_ref, behind_ref, halo_ref, grouped_ref, single_ref,
    table_ref, out_ref, planar_ref,
):
    groups = across_ref.shape[0]
    variant = jnp.minimum(tile_ref[0], 1)
    weights = grouped_ref[variant]
    stacked = jnp.concatenate([behind_ref[groups], halo_ref[groups]], axis=0)
    behind = dot(single_ref[variant], stacked)
    behind = jnp.where(first_ref[0] == 0, jnp.zeros_like(behind), behind)
    planar_ref[0] = behind.astype(jnp.bfloat16)
    for g in range(groups):
        stacked = jnp.concatenate([across_ref[g], halo_ref[g]], axis=0)
        planar = dot(weights, stacked).astype(jnp.bfloat16)
        planar_ref[1 + g * GROUP : 1 + (g + 1) * GROUP] = planar.reshape(GROUP, 16, HALF)
    table = table_ref[...]
    sections = groups * GROUP // 2
    for m in range(sections // 16):
        made = []
        for s in range(m * 16, (m + 1) * 16):
            before = planar_ref[2 * s].astype(jnp.float32)
            middle = planar_ref[2 * s + 1].astype(jnp.float32)
            after = planar_ref[2 * s + 2].astype(jnp.float32)
            made.append(((before + 2.0 * middle + after) * 0.25).astype(jnp.bfloat16))
        rows = jnp.concatenate(made, axis=0)
        out_ref[:, m * HALF : (m + 1) * HALF] = dot_nt(table, rows).astype(jnp.bfloat16)


def row_spectra(tile, first, across, behind, halo, grouped, single, table):
    groups = across.shape[0]
    rows = groups * GROUP // 2 * 16
    return pl.pallas_call(
        section_kernel,
        in_specs=[whole(pltpu.SMEM), whole(pltpu.SMEM)] + [whole()] * 6,
        out_specs=whole(),
        out_shape=jax.ShapeDtypeStruct((HALF, rows), jnp.bfloat16),
        scratch_shapes=[pltpu.VMEM((groups * GROUP + 1, 16, HALF), jnp.bfloat16)],
        compiler_params=params(),
        name="row_spectra",
    )(tile, first, across, behind, halo, grouped, single, table)


def cross_kernel(
    tile_ref, section_ref, row_ref, extent_ref, owner_ref, spectra_ref, table_ref,
    out_ref, held_ref, band_ref, count_ref,
):
    pairs = owner_ref.shape[0]
    blocks = spectra_ref.shape[2] // 128
    lane = lax.broadcasted_iota(jnp.int32, (16, 128), 1)
    for k in range(blocks):
        for h in range(2):
            a = [
                spectra_ref[8 * h + t, :, 128 * k : 128 * (k + 1)].astype(jnp.float32)
                for t in range(8)
            ]
            for bit in (1, 2, 4):
                low = (lane // 16) & bit == 0
                for i in range(8):
                    if i & bit:
                        continue
                    j = i + bit
                    first = jnp.where(low, a[i], pltpu.roll(a[j], 16 * bit, 1))
                    second = jnp.where(low, pltpu.roll(a[i], 128 - 16 * bit, 1), a[j])
                    a[i], a[j] = first, second
            for s in range(8):
                held_ref[8 * k + s, h] = a[s]

    out_ref[...] = jnp.zeros_like(out_ref)
    for o in range(TILES):
        count_ref[o] = 0

    def cut(n, _):
        extent = extent_ref[n]
        for side in range(2):
            which = section_ref[side, n]
            start = row_ref[side, n] + 1
            low = held_ref[which, 0]
            high = held_ref[which, 1]
            from_low = (lane >= start) | (lane < start - 128)
            mixed = jnp.where(from_low, low, high)
            turned = pltpu.roll(mixed, lax.rem(256 - start, 128), 1)
            band = jnp.where(lane < extent, turned, 0.0)
            band_ref[2 * n + side] = band.astype(jnp.bfloat16)
        return 0

    lax.fori_loop(0, pairs, cut, 0, unroll=4)

    eight = (FREQS, 128)
    column = lax.broadcasted_iota(jnp.int32, eight, 1)
    special = (lax.broadcasted_iota(jnp.int32, eight, 0) == 0) & (tile_ref[0] == 0)
    upper = column > BAND // 2
    batch = 8

    def cross(step, _):
        bands = band_ref[pl.ds(step * 2 * batch, 2 * batch)].reshape(2 * batch * 16, 128)
        full = dot(bands, table_ref[...])
        for p in range(batch):
            real, imag, edge_real, edge_imag = [], [], [], []
            for side in range(2):
                at = (2 * p + side) * 16
                cos_re = full[at : at + 8, :128]
                sin_re = full[at : at + 8, 128:]
                cos_im = full[at + 8 : at + 16, :128]
                sin_im = full[at + 8 : at + 16, 128:]
                real.append(cos_re + jnp.where(special, 0.0, sin_im))
                imag.append(jnp.where(special, 0.0, cos_im) - sin_re)
                edge_real.append(cos_im)
                edge_imag.append(-sin_im)
            cross_real = real[0] * real[1] + imag[0] * imag[1]
            cross_imag = imag[0] * real[1] - real[0] * imag[1]
            last_real = edge_real[0] * edge_real[1] + edge_imag[0] * edge_imag[1]
            last_imag = edge_imag[0] * edge_real[1] - edge_real[0] * edge_imag[1]
            first_slot = jnp.where(special & upper, cross_imag, cross_real)
            packed = jnp.where(upper, last_imag, last_real)
            second_slot = jnp.where(special, packed, cross_imag)
            n = step * batch + p
            owner = owner_ref[n]
            slot = count_ref[owner]
            count_ref[owner] = slot + 1
            both = jnp.concatenate([first_slot, second_slot], axis=0)
            out_ref[owner * OWN_CAP + slot] = both.astype(jnp.bfloat16)
        return 0

    lax.fori_loop(0, pairs // batch, cross, 0)


def cross_spectra(tile, sections, rows, extents, owners, spectra, table):
    pairs = owners.shape[0]
    held = spectra.shape[2] // 16
    return pl.pallas_call(
        cross_kernel,
        in_specs=[whole(pltpu.SMEM)] * 5 + [whole()] * 2,
        out_specs=whole(),
        out_shape=jax.ShapeDtypeStruct((TILES * OWN_CAP, 16, 128), jnp.bfloat16),
        scratch_shapes=[
            pltpu.VMEM((held, 2, 16, 128), jnp.float32),
            pltpu.VMEM((2 * pairs, 16, 128), jnp.bfloat16),
            pltpu.SMEM((TILES,), jnp.int32),
        ],
        compiler_params=params(),
        name="cross_spectra",
    )(tile, sections, rows, extents, owners, spectra, table)


def surface_kernel(
    tile_ref, owner_ref, cross_ref, reversal_ref, column_ref, row_ref, out_ref,
    turned_ref, count_ref,
):
    step = pl.program_id(0)
    slots = out_ref.shape[0]
    lane = lax.broadcasted_iota(jnp.int32, (FREQS, 128), 1)
    top = lax.broadcasted_iota(jnp.int32, (FREQS, 128), 0) == 0

    @pl.when(step == 0)
    def _():
        turned = dot(cross_ref[0].reshape(OWN_CAP * 16, 128), reversal_ref[...])
        turned_ref[...] = turned.reshape(OWN_CAP, 16, 128)
        tile = tile_ref[0]
        count_ref[0] = lax.fori_loop(
            0,
            owner_ref.shape[0],
            lambda n, c: c + jnp.where(owner_ref[n] == tile, 1, 0),
            0,
            unroll=8,
        )

    def unpack(packed, turned):
        real = jnp.where(lane <= BAND // 2, packed, turned)
        ends = (lane == 0) | (lane == BAND // 2)
        imag = jnp.where(lane > BAND // 2, packed, jnp.where(ends, 0.0, -turned))
        return real, imag

    def rounded(value, divisor):
        return (value / divisor).astype(jnp.bfloat16).astype(jnp.float32)

    for k in range(slots):
        slot = step * slots + k

        @pl.when(slot < count_ref[0])
        def _():
            block = cross_ref[:, slot].astype(jnp.float32)
            real = block[:, :8, :].reshape(128, 128)
            imag = block[:, 8:, :].reshape(128, 128)
            turned = turned_ref[slot]
            real_0, imag_0 = unpack(real[:8], turned[:8])
            real_n, imag_n = unpack(imag[:8], turned[8:])
            real = jnp.concatenate([jnp.where(top, real_0, real[:8]), real[8:]], axis=0)
            imag = jnp.concatenate([jnp.where(top, imag_0, imag[:8]), imag[8:]], axis=0)
            size = jnp.sqrt(real * real + imag * imag)
            size_n = jnp.sqrt(real_n * real_n + imag_n * imag_n)
            ends = jnp.where(top, size_n - size[:8], 0.0)
            total = 2.0 * jnp.sum(size) + jnp.sum(ends)
            mean_level = total / (BAND * HALF) + 1e-06
            divisor = size + mean_level
            norm_real = rounded(real, divisor)
            norm_imag = rounded(imag, divisor)
            divisor_n = size_n + mean_level
            last = rounded(real_n, divisor_n) - rounded(imag_n, divisor_n)
            zero = norm_real[:8] - norm_imag[:8]
            stacked = jnp.concatenate(
                [
                    jnp.where(top, zero, norm_real[:8]),
                    norm_real[8:],
                    jnp.where(top, last, norm_imag[:8]),
                    norm_imag[8:],
                ],
                axis=0,
            ).astype(jnp.bfloat16)
            full = dot_nt(column_ref[...], stacked)
            edge = lax.broadcasted_iota(jnp.int32, (128, 128), 1) == 0
            cos_re, cos_im = full[:128, :128], full[:128, 128:]
            sin_re, sin_im = full[128:, :128], full[128:, 128:]
            col_real = cos_re + jnp.where(edge, sin_re, -sin_im)
            col_imag = cos_im + jnp.where(edge, sin_im, sin_re)
            col = jnp.concatenate([col_real, col_imag], axis=1).astype(jnp.bfloat16)
            out_ref[k] = dot(col, row_ref[...]).astype(jnp.bfloat16)

        @pl.when(slot >= count_ref[0])
        def _():
            out_ref[k] = jnp.zeros((BAND, HALF), jnp.bfloat16)


def surfaces(tile, owners, cross, back, column, row):
    step = 3
    return pl.pallas_call(
        surface_kernel,
        grid=(OWN_CAP // step,),
        in_specs=[whole(pltpu.SMEM)] * 2 + [whole()] * 4,
        out_specs=pl.BlockSpec((step, BAND, HALF), lambda g: (g, 0, 0)),
        out_shape=jax.ShapeDtypeStruct((OWN_CAP, BAND, HALF), jnp.bfloat16),
        scratch_shapes=[
            pltpu.VMEM((OWN_CAP, 16, 128), jnp.float32),
            pltpu.SMEM((1,), jnp.int32),
        ],
        compiler_params=params(),
        name="surfaces",
    )(tile, owners, cross, back, column, row)


def per_device(raw_planes, pair_sections, pair_rows, pair_extent, pair_owner):
    tile = lax.axis_index("tile").astype(jnp.int32).reshape(1)
    slab = lax.axis_index("plane").astype(jnp.int32).reshape(1)
    slabs = lax.axis_size("plane")
    planes = raw_planes.shape[0]
    owners = pair_owner[:, 0]

    table = blur_matrix()
    behind = lax.ppermute(
        raw_planes[planes - 1], "plane", [(s, s + 1) for s in range(slabs - 1)]
    )
    across, edges = blur_across(raw_planes, table, halo_select())
    edges = blur_behind(behind, table, edges)
    halo = lax.ppermute(edges, "tile", [(t, (t + 1) % TILES) for t in range(TILES)])
    grouped, single = column_tables()
    spectra = row_spectra(
        tile, slab, across, edges, halo, grouped, single, row_transform_table()
    )
    spectra = lax.all_to_all(
        spectra.reshape(TILES, 16, spectra.shape[1]), "tile", 0, 0, tiled=True
    )

    cos_band, sin_band = dft_tables(BAND)
    cross = cross_spectra(
        tile,
        pair_sections.T,
        pair_rows.T,
        pair_extent,
        owners,
        spectra,
        np.concatenate([cos_band, sin_band], axis=1),
    )
    cross = lax.all_to_all(
        cross.reshape(TILES, OWN_CAP * 16, 128), "tile", 0, 0, tiled=True
    )
    return surfaces(
        tile,
        owners,
        cross.reshape(TILES, OWN_CAP, 16, 128),
        reversal(),
        np.concatenate([cos_band, sin_band], axis=0),
        row_inverse_table(),
    )


def solution(mesh):
    return jax.shard_map(
        per_device,
        mesh=mesh,
        in_specs=(
            P("plane", "tile", None),
            P("plane", None),
            P("plane", None),
            P("plane"),
            P("plane", None),
        ),
        out_specs=P(("plane", "tile"), None, None),
        check_vma=False,
    )
```

```python
import functools
import math

import jax
import jax.numpy as jnp
import numpy as np
from jax import lax
from jax.experimental import pallas as pl
from jax.experimental.pallas import tpu as pltpu
from jax.sharding import PartitionSpec as P

BAND = 128
OWN_CAP = 12
FACE = 512
HALF = 256
TILES = 16
FREQS = 8
GROUP = 8
VMEM_LIMIT = 24 * 1024 * 1024


def whole(space=pltpu.VMEM):
    return pl.BlockSpec(memory_space=space)


def params(**kw):
    return pltpu.CompilerParams(vmem_limit_bytes=VMEM_LIMIT, **kw)


def blur_weight(offset):
    offset = abs(offset)
    return (6.0, 4.0, 1.0)[offset] / 16.0 if offset <= 2 else 0.0


def blur_matrix():
    table = np.zeros((FACE, HALF), np.float32)
    for c in range(FACE):
        for j in range(HALF):
            if abs(c - 2 * j) <= 2:
                table[c, j] = blur_weight(c - 2 * j)
    return table.astype(jnp.bfloat16)


def dft_tables(length):
    indices = np.arange(length)
    phases = indices[:, None] * indices[None, :] % length
    angles = phases.astype(np.float32) * np.float32(2.0 * math.pi / length)
    factor = np.float32(1.0 / math.sqrt(length))
    return (
        (np.cos(angles) * factor).astype(jnp.bfloat16),
        (np.sin(angles) * factor).astype(jnp.bfloat16),
    )


def column_weights(first_tile):
    local = np.zeros((16, 32), np.float32)
    halo = np.zeros((16, 4), np.float32)
    for i in range(16):
        for c in range(32):
            local[i, c] = blur_weight(c + 2 - 2 * i)
        for h in range(4):
            halo[i, h] = blur_weight(h - 2 - 2 * i)
    if first_tile:
        local[0, 0] = 0.0
        halo[1, :] = 0.0
    return local, halo


def column_tables():
    grouped = np.zeros((2, GROUP * 16, GROUP * 36), np.float32)
    single = np.zeros((2, 16, 64), np.float32)
    for variant in (0, 1):
        local, halo = column_weights(variant == 0)
        for q in range(GROUP):
            rows = slice(q * 16, q * 16 + 16)
            grouped[variant, rows, q * 32 : q * 32 + 32] = local
            at = GROUP * 32 + q * 4
            grouped[variant, rows, at : at + 4] = halo
        single[variant, :, :32] = local
        single[variant, :, 60:64] = halo
    return grouped.astype(jnp.bfloat16), single.astype(jnp.bfloat16)


def row_transform_table():
    cos_half, sin_half = dft_tables(HALF)
    table = np.zeros((HALF, HALF), np.float32)
    for d in range(TILES):
        for f in range(FREQS):
            v = d * FREQS + f
            table[d * 16 + f] = cos_half[v]
            if v:
                table[d * 16 + FREQS + f] = -sin_half[v].astype(np.float32)
            else:
                table[d * 16 + FREQS + f] = cos_half[HALF // 2]
    return table.astype(jnp.bfloat16)


def row_inverse_table():
    cos_half, sin_half = dft_tables(HALF)
    table = np.zeros((HALF, HALF), np.float32)
    for v in range(HALF // 2):
        table[v] = cos_half[v].astype(np.float32) * (2.0 if v else 1.0)
        if v:
            table[HALF // 2 + v] = sin_half[v].astype(np.float32) * -2.0
        else:
            table[HALF // 2] = cos_half[HALF // 2]
    return table.astype(jnp.bfloat16)


def reversal():
    table = np.zeros((BAND, BAND), np.float32)
    for u in range(BAND):
        table[(BAND - u) % BAND, u] = 1.0
    return table.astype(jnp.bfloat16)


def dot(a, b):
    return jnp.dot(a, b, preferred_element_type=jnp.float32)


def dot_nt(a, b):
    return lax.dot_general(
        a, b, (((1,), (1,)), ((), ())), preferred_element_type=jnp.float32
    )


def edge_kernel(raw_ref, table_hbm, edge_ref, strip_ref, table_ref, sems):
    planes = raw_ref.shape[0]
    part = 32
    copies = [pltpu.make_async_copy(table_hbm, table_ref, sems.at[0])]
    for k in range(planes // part):
        held = pl.ds(k * part, part)
        copies.append(
            pltpu.make_async_copy(
                raw_ref.at[held, pl.ds(24, 8), :], strip_ref.at[held], sems.at[k + 1]
            )
        )
    for copy in copies:
        copy.start()
    shape = (part * 4, part * 8)
    row = lax.broadcasted_iota(jnp.int32, shape, 0)
    source = lax.broadcasted_iota(jnp.int32, shape, 1)
    select = jnp.where(source == (row >> 2) * 8 + 4 + (row & 3), 1.0, 0.0)
    select = select.astype(jnp.bfloat16)
    copies[0].wait()
    for k in range(planes // part):
        copies[k + 1].wait()
        cells = strip_ref[k * part : (k + 1) * part].reshape(part * 8, FACE)
        across = dot(cells, table_ref[...]).astype(jnp.bfloat16)
        edges = dot(select, across).astype(jnp.bfloat16)
        at = k * (part // GROUP)
        edge_ref[at : at + part // GROUP] = edges.reshape(part // GROUP, GROUP * 4, HALF)


def blur_edges(raw, table):
    planes = raw.shape[0]
    return pl.pallas_call(
        edge_kernel,
        in_specs=[whole(pltpu.HBM)] * 2,
        out_specs=whole(),
        out_shape=jax.ShapeDtypeStruct(
            (planes // GROUP + 1, GROUP * 4, HALF), jnp.bfloat16
        ),
        scratch_shapes=[
            pltpu.VMEM((planes, 8, FACE), jnp.bfloat16),
            pltpu.VMEM((FACE, HALF), jnp.bfloat16),
            pltpu.SemaphoreType.DMA((planes // 32 + 1,)),
        ],
        compiler_params=params(),
        cost_estimate=pl.CostEstimate(
            flops=2 * planes * 8 * FACE * HALF,
            bytes_accessed=planes * 8 * FACE * 2,
            transcendentals=0,
        ),
        name="blur_edges",
    )(raw, table)


def across_kernel(raw_ref, table_hbm, across_ref, cells_ref, table_ref, sems):
    planes = raw_ref.shape[0]
    part = 16
    copies = [pltpu.make_async_copy(table_hbm, table_ref, sems.at[0])]
    for k in range(planes // part):
        held = pl.ds(k * part, part)
        copies.append(
            pltpu.make_async_copy(raw_ref.at[held], cells_ref.at[held], sems.at[k + 1])
        )
    for copy in copies:
        copy.start()
    copies[0].wait()
    per = part // GROUP
    for k in range(planes // part):
        copies[k + 1].wait()
        cells = cells_ref[k * part : (k + 1) * part].reshape(part * 32, FACE)
        across = dot(cells, table_ref[...]).astype(jnp.bfloat16)
        across_ref[k * per : (k + 1) * per] = across.reshape(per, GROUP * 32, HALF)


def blur_across(raw, table):
    planes = raw.shape[0]
    return pl.pallas_call(
        across_kernel,
        in_specs=[whole(pltpu.HBM)] * 2,
        out_specs=whole(),
        out_shape=jax.ShapeDtypeStruct((planes // GROUP, GROUP * 32, HALF), jnp.bfloat16),
        scratch_shapes=[
            pltpu.VMEM((planes, 32, FACE), jnp.bfloat16),
            pltpu.VMEM((FACE, HALF), jnp.bfloat16),
            pltpu.SemaphoreType.DMA((planes // 16 + 1,)),
        ],
        compiler_params=params(),
        cost_estimate=pl.CostEstimate(
            flops=2 * planes * 32 * FACE * HALF,
            bytes_accessed=planes * 32 * (FACE + HALF) * 2,
            transcendentals=0,
        ),
        name="blur_across",
    )(raw, table)


def behind_kernel(plane_ref, table_ref, edges_in_ref, edge_ref):
    edge_ref[0] = dot(plane_ref[...], table_ref[...]).astype(jnp.bfloat16)


def blur_behind(plane, table, edges):
    last = edges.shape[0] - 1
    return pl.pallas_call(
        behind_kernel,
        grid=(1,),
        in_specs=[
            pl.BlockSpec((32, FACE), lambda g: (0, 0)),
            pl.BlockSpec((FACE, HALF), lambda g: (0, 0)),
            pl.BlockSpec(memory_space=pl.ANY),
        ],
        out_specs=pl.BlockSpec((1, 32, HALF), lambda g: (last, 0, 0)),
        out_shape=jax.ShapeDtypeStruct(edges.shape, jnp.bfloat16),
        input_output_aliases={2: 0},
        compiler_params=params(),
        name="blur_behind",
    )(plane, table, edges)


def section_kernel(
    tile_ref, across_ref, behind_ref, halo_ref, grouped_ref, single_ref,
    table_ref, out_ref, planar_ref,
):
    groups = across_ref.shape[0]
    variant = jnp.minimum(tile_ref[0], 1)
    weights = grouped_ref[variant]
    stacked = jnp.concatenate([behind_ref[groups], halo_ref[groups]], axis=0)
    behind = dot(single_ref[variant], stacked)
    planar_ref[0] = behind.astype(jnp.bfloat16)
    for g in range(groups):
        stacked = jnp.concatenate([across_ref[g], halo_ref[g]], axis=0)
        planar = dot(weights, stacked).astype(jnp.bfloat16)
        planar_ref[1 + g * GROUP : 1 + (g + 1) * GROUP] = planar.reshape(GROUP, 16, HALF)
    table = table_ref[...]
    sections = groups * GROUP // 2
    for m in range(sections // 16):
        made = []
        for s in range(m * 16, (m + 1) * 16):
            before = planar_ref[2 * s].astype(jnp.float32)
            middle = planar_ref[2 * s + 1].astype(jnp.float32)
            after = planar_ref[2 * s + 2].astype(jnp.float32)
            made.append(((before + 2.0 * middle + after) * 0.25).astype(jnp.bfloat16))
        rows = jnp.concatenate(made, axis=0)
        out_ref[:, m * HALF : (m + 1) * HALF] = dot_nt(table, rows).astype(jnp.bfloat16)


def row_spectra(tile, across, behind, halo, grouped, single, table):
    groups = across.shape[0]
    rows = groups * GROUP // 2 * 16
    return pl.pallas_call(
        section_kernel,
        in_specs=[whole(pltpu.SMEM)] + [whole()] * 6,
        out_specs=whole(),
        out_shape=jax.ShapeDtypeStruct((HALF, rows), jnp.bfloat16),
        scratch_shapes=[pltpu.VMEM((groups * GROUP + 1, 16, HALF), jnp.bfloat16)],
        compiler_params=params(),
        name="row_spectra",
    )(tile, across, behind, halo, grouped, single, table)


def cross_kernel(
    tile_ref, meta_ref, spectra_ref, table_ref, out_ref, held_ref, band_ref
):
    pairs = meta_ref.shape[1]
    blocks = spectra_ref.shape[2] // 128
    lane = lax.broadcasted_iota(jnp.int32, (16, 128), 1)
    out_ref[...] = jnp.zeros_like(out_ref)
    for k in range(blocks):
        for h in range(2):
            a = [
                spectra_ref[8 * h + t, :, 128 * k : 128 * (k + 1)].astype(jnp.float32)
                for t in range(8)
            ]
            for bit in (1, 2, 4):
                low = (lane // 16) & bit == 0
                for i in range(8):
                    if i & bit:
                        continue
                    j = i + bit
                    first = jnp.where(low, a[i], pltpu.roll(a[j], 16 * bit, 1))
                    second = jnp.where(low, pltpu.roll(a[i], 128 - 16 * bit, 1), a[j])
                    a[i], a[j] = first, second
            for s in range(8):
                held_ref[8 * k + s, h] = a[s]

    batch = 8
    steps = pairs // batch
    eight = (FREQS, 128)
    column = lax.broadcasted_iota(jnp.int32, eight, 1)
    special = (lax.broadcasted_iota(jnp.int32, eight, 0) == 0) & (tile_ref[0] == 0)
    upper = column > BAND // 2

    def cut(step, buffer):
        for p in range(batch):
            n = step * batch + p
            live = lane < meta_ref[4, n]
            for side in range(2):
                which = meta_ref[side, n]
                start = meta_ref[2 + side, n]
                from_low = (lane >= start) | (lane < start - 128)
                mixed = jnp.where(from_low, held_ref[which, 0], held_ref[which, 1])
                turned = pltpu.roll(mixed, (256 - start) & 127, 1)
                band = jnp.where(live, turned, 0.0)
                band_ref[buffer, 2 * p + side] = band.astype(jnp.bfloat16)

    def cross(step, buffer):
        bands = band_ref[buffer].reshape(2 * batch * 16, 128)
        full = dot(bands, table_ref[...])
        for p in range(batch):
            real, imag, edge_real, edge_imag = [], [], [], []
            for side in range(2):
                at = (2 * p + side) * 16
                cos_re = full[at : at + 8, :128]
                sin_re = full[at : at + 8, 128:]
                cos_im = full[at + 8 : at + 16, :128]
                sin_im = full[at + 8 : at + 16, 128:]
                real.append(cos_re + jnp.where(special, 0.0, sin_im))
                imag.append(jnp.where(special, 0.0, cos_im) - sin_re)
                edge_real.append(cos_im)
                edge_imag.append(-sin_im)
            cross_real = real[0] * real[1] + imag[0] * imag[1]
            cross_imag = imag[0] * real[1] - real[0] * imag[1]
            last_real = edge_real[0] * edge_real[1] + edge_imag[0] * edge_imag[1]
            last_imag = edge_imag[0] * edge_real[1] - edge_real[0] * edge_imag[1]
            first_slot = jnp.where(special & upper, cross_imag, cross_real)
            packed = jnp.where(upper, last_imag, last_real)
            second_slot = jnp.where(special, packed, cross_imag)
            both = jnp.concatenate([first_slot, second_slot], axis=0)
            out_ref[meta_ref[5, step * batch + p]] = both.astype(jnp.bfloat16)

    cut(0, 0)

    def body(step, _):
        cross(step, step & 1)
        cut(step + 1, (step + 1) & 1)
        return 0

    lax.fori_loop(0, steps - 1, body, 0)
    cross(steps - 1, (steps - 1) & 1)


def pair_table(sections, rows, extents, owners):
    position = jnp.arange(owners.shape[0], dtype=jnp.int32)
    earlier = (owners[:, None] == owners[None, :]) & (position[None, :] < position[:, None])
    slots = jnp.sum(earlier.astype(jnp.int32), axis=1)
    places = owners * OWN_CAP + slots
    return jnp.concatenate([sections.T, rows.T + 1, extents[None], places[None]], axis=0)


def cross_spectra(tile, meta, spectra, table):
    held = spectra.shape[2] // 16
    return pl.pallas_call(
        cross_kernel,
        in_specs=[whole(pltpu.SMEM)] * 2 + [whole()] * 2,
        out_specs=whole(),
        out_shape=jax.ShapeDtypeStruct((TILES * OWN_CAP, 16, 128), jnp.bfloat16),
        scratch_shapes=[
            pltpu.VMEM((held, 2, 16, 128), jnp.float32),
            pltpu.VMEM((2, 16, 16, 128), jnp.bfloat16),
        ],
        compiler_params=params(),
        name="cross_spectra",
    )(tile, meta, spectra, table)


def surface_kernel(cross_ref, reversal_ref, column_ref, row_ref, out_ref, turned_ref):
    step = pl.program_id(0)
    slots = out_ref.shape[0]
    lane = lax.broadcasted_iota(jnp.int32, (FREQS, 128), 1)
    top = lax.broadcasted_iota(jnp.int32, (FREQS, 128), 0) == 0
    edge = lax.broadcasted_iota(jnp.int32, (128, 128), 1) == 0
    upper = lane > BAND // 2
    ends = (lane == 0) | (lane == BAND // 2)

    @pl.when(step == 0)
    def _():
        turned = dot(cross_ref[0].reshape(OWN_CAP * 16, 128), reversal_ref[...])
        turned_ref[...] = turned.reshape(OWN_CAP, 16, 128)

    def unpack(packed, turned):
        real = jnp.where(upper, turned, packed)
        imag = jnp.where(upper, packed, jnp.where(ends, 0.0, -turned))
        return real, imag

    def rounded(value):
        return value.astype(jnp.bfloat16).astype(jnp.float32)

    def replaced(row, rows):
        return jnp.concatenate([jnp.where(top, row, rows[:8]), rows[8:]], axis=0)

    columns = []
    for k in range(slots):
        slot = step * slots + k
        block = cross_ref[:, slot].astype(jnp.float32)
        real = block[:, :8, :].reshape(128, 128)
        imag = block[:, 8:, :].reshape(128, 128)
        turned = turned_ref[slot]
        real_0, imag_0 = unpack(real[:8], turned[:8])
        real_n, imag_n = unpack(imag[:8], turned[8:])
        real = replaced(real_0, real)
        imag = replaced(imag_0, imag)
        size = jnp.sqrt(real * real + imag * imag)
        size_n = jnp.sqrt(real_n * real_n + imag_n * imag_n)
        total = 2.0 * jnp.sum(size.reshape(16, 8, 128), axis=0)
        total = jnp.sum(total + jnp.where(top, size_n - size[:8], 0.0))
        mean_level = total / (BAND * HALF) + 1e-06
        scale = 1.0 / (size + mean_level)
        scale_n = 1.0 / (size_n + mean_level)
        norm_real = real * scale
        norm_imag = imag * scale
        zero = rounded(norm_real[:8]) - rounded(norm_imag[:8])
        last = rounded(real_n * scale_n) - rounded(imag_n * scale_n)
        stacked = jnp.concatenate(
            [replaced(zero, norm_real), replaced(last, norm_imag)], axis=0
        ).astype(jnp.bfloat16)
        full = dot_nt(column_ref[...], stacked)
        cos_re, cos_im = full[:128, :128], full[:128, 128:]
        sin_re, sin_im = full[128:, :128], full[128:, 128:]
        col_real = cos_re + jnp.where(edge, sin_re, -sin_im)
        col_imag = cos_im + jnp.where(edge, sin_im, sin_re)
        col = jnp.concatenate([col_real, col_imag], axis=1)
        columns.append(col.astype(jnp.bfloat16))
    made = dot(jnp.concatenate(columns, axis=0), row_ref[...]).astype(jnp.bfloat16)
    out_ref[...] = made.reshape(slots, BAND, HALF)


def surfaces(cross, back, column, row):
    step = 3
    return pl.pallas_call(
        surface_kernel,
        grid=(OWN_CAP // step,),
        in_specs=[whole()] * 4,
        out_specs=pl.BlockSpec((step, BAND, HALF), lambda g: (g, 0, 0)),
        out_shape=jax.ShapeDtypeStruct((OWN_CAP, BAND, HALF), jnp.bfloat16),
        scratch_shapes=[pltpu.VMEM((OWN_CAP, 16, 128), jnp.float32)],
        compiler_params=params(),
        name="surfaces",
    )(cross, back, column, row)


def per_device(raw_planes, pair_sections, pair_rows, pair_extent, pair_owner):
    tile = lax.axis_index("tile").astype(jnp.int32).reshape(1)
    slabs = lax.axis_size("plane")
    planes = raw_planes.shape[0]
    owners = pair_owner[:, 0]

    table = pltpu.with_memory_space_constraint(jnp.asarray(blur_matrix()), pltpu.HBM)
    raw_held = pltpu.with_memory_space_constraint(raw_planes, pltpu.HBM)
    behind = lax.ppermute(
        raw_planes[planes - 1], "plane", [(s, s + 1) for s in range(slabs - 1)]
    )
    edges = blur_behind(behind, blur_matrix(), blur_edges(raw_held, table))
    halo = lax.ppermute(edges, "tile", [(t, (t + 1) % TILES) for t in range(TILES)])
    across = blur_across(raw_held, table)
    grouped, single = column_tables()
    spectra = row_spectra(
        tile, across, edges, halo, grouped, single, row_transform_table()
    )
    spectra = lax.all_to_all(
        spectra.reshape(TILES, 16, spectra.shape[1]), "tile", 0, 0, tiled=True
    )

    cos_band, sin_band = dft_tables(BAND)
    meta = pair_table(pair_sections, pair_rows, pair_extent, owners)
    cross = cross_spectra(
        tile, meta, spectra, np.concatenate([cos_band, sin_band], axis=1)
    )
    cross = lax.all_to_all(
        cross.reshape(TILES, OWN_CAP * 16, 128), "tile", 0, 0, tiled=True
    )
    return surfaces(
        cross.reshape(TILES, OWN_CAP, 16, 128),
        reversal(),
        np.concatenate([cos_band, sin_band], axis=0),
        row_inverse_table(),
    )


def solution(mesh):
    return jax.shard_map(
        per_device,
        mesh=mesh,
        in_specs=(
            P("plane", "tile", None),
            P("plane", None),
            P("plane", None),
            P("plane"),
            P("plane", None),
        ),
        out_specs=P(("plane", "tile"), None, None),
        check_vma=False,
    )
```

```python
import math

import jax
import jax.numpy as jnp
import numpy as np
from jax import lax
from jax.experimental import pallas as pl
from jax.experimental.pallas import tpu as pltpu
from jax.sharding import PartitionSpec as P

BAND = 128
OWN_CAP = 12
FACE = 512
HALF = 256
TILES = 16
DEPTH = 8
FREQS = 8
GROUP = 8
VMEM_LIMIT = 24 * 1024 * 1024


def whole(space=pltpu.VMEM):
    return pl.BlockSpec(memory_space=space)


def params(**kw):
    return pltpu.CompilerParams(vmem_limit_bytes=VMEM_LIMIT, **kw)


def blur_weight(offset):
    offset = abs(offset)
    return (6.0, 4.0, 1.0)[offset] / 16.0 if offset <= 2 else 0.0


def blur_matrix():
    table = np.zeros((FACE, HALF), np.float32)
    for c in range(FACE):
        for j in range(HALF):
            if abs(c - 2 * j) <= 2:
                table[c, j] = blur_weight(c - 2 * j)
    return table.astype(jnp.bfloat16)


def dft_tables(length):
    indices = np.arange(length)
    phases = indices[:, None] * indices[None, :] % length
    angles = phases.astype(np.float32) * np.float32(2.0 * math.pi / length)
    factor = np.float32(1.0 / math.sqrt(length))
    return (
        (np.cos(angles) * factor).astype(jnp.bfloat16),
        (np.sin(angles) * factor).astype(jnp.bfloat16),
    )


def column_weights(first_tile):
    local = np.zeros((16, 32), np.float32)
    halo = np.zeros((16, 4), np.float32)
    for i in range(16):
        for c in range(32):
            local[i, c] = blur_weight(c + 2 - 2 * i)
        for h in range(4):
            halo[i, h] = blur_weight(h - 2 - 2 * i)
    if first_tile:
        local[0, 0] = 0.0
        halo[1, :] = 0.0
    return local, halo


def column_tables():
    grouped = np.zeros((2, GROUP * 16, GROUP * 36), np.float32)
    single = np.zeros((2, 16, 40), np.float32)
    for variant in (0, 1):
        local, halo = column_weights(variant == 0)
        for q in range(GROUP):
            rows = slice(q * 16, q * 16 + 16)
            grouped[variant, rows, q * 32 : q * 32 + 32] = local
            at = GROUP * 32 + q * 4
            grouped[variant, rows, at : at + 4] = halo
        single[variant, :, :32] = local
        single[variant, :, 36:40] = halo
    return grouped.astype(jnp.bfloat16), single.astype(jnp.bfloat16)


def row_transform_table():
    cos_half, sin_half = dft_tables(HALF)
    table = np.zeros((HALF, HALF), np.float32)
    for d in range(TILES):
        for f in range(FREQS):
            v = d * FREQS + f
            table[d * 16 + f] = cos_half[v]
            if v:
                table[d * 16 + FREQS + f] = -sin_half[v].astype(np.float32)
            else:
                table[d * 16 + FREQS + f] = cos_half[HALF // 2]
    return table.astype(jnp.bfloat16)


def row_inverse_table():
    cos_half, sin_half = dft_tables(HALF)
    table = np.zeros((HALF, HALF), np.float32)
    for v in range(HALF // 2):
        table[v] = cos_half[v].astype(np.float32) * (2.0 if v else 1.0)
        if v:
            table[HALF // 2 + v] = sin_half[v].astype(np.float32) * -2.0
        else:
            table[HALF // 2] = cos_half[HALF // 2]
    return table.astype(jnp.bfloat16)


def reversal():
    table = np.zeros((BAND, BAND), np.float32)
    for u in range(BAND):
        table[(BAND - u) % BAND, u] = 1.0
    return table.astype(jnp.bfloat16)


def dot(a, b):
    return jnp.dot(a, b, preferred_element_type=jnp.float32)


def dot_nt(a, b):
    return lax.dot_general(
        a, b, (((1,), (1,)), ((), ())), preferred_element_type=jnp.float32
    )


def across_kernel(raw_ref, table_hbm, across_ref, edge_ref, cells_ref, table_ref, sems):
    planes = raw_ref.shape[0]
    part = 16
    parts = planes // part
    ahead = 3

    def copy(k):
        held = pl.ds(k * part, part)
        return pltpu.make_async_copy(raw_ref.at[held], cells_ref.at[held], sems.at[k + 1])

    table_copy = pltpu.make_async_copy(table_hbm, table_ref, sems.at[0])
    table_copy.start()
    for k in range(ahead):
        copy(k).start()
    table_copy.wait()
    per = part // GROUP
    upper = lax.broadcasted_iota(jnp.int32, (8, HALF), 0) < 4
    for k in range(parts):
        copy(k).wait()
        if k + ahead < parts:
            copy(k + ahead).start()
        cells = cells_ref[k * part : (k + 1) * part].reshape(part * 32, FACE)
        across = dot(cells, table_ref[...])
        edges = []
        for q in range(0, part, 2):
            first = across[q * 32 + 24 : q * 32 + 32]
            second = across[q * 32 + 56 : q * 32 + 64]
            edges.append(jnp.where(upper, pltpu.roll(first, 4, 0), second))
        edges = jnp.concatenate(edges, axis=0).astype(jnp.bfloat16)
        edge_ref[k * per : (k + 1) * per] = edges.reshape(per, GROUP * 4, HALF)
        across = across.astype(jnp.bfloat16)
        across_ref[k * per : (k + 1) * per] = across.reshape(per, GROUP * 32, HALF)


def blur_across(raw, table):
    planes = raw.shape[0]
    groups = planes // GROUP
    return pl.pallas_call(
        across_kernel,
        in_specs=[whole(pltpu.HBM)] * 2,
        out_specs=[whole()] * 2,
        out_shape=[
            jax.ShapeDtypeStruct((groups, GROUP * 32, HALF), jnp.bfloat16),
            jax.ShapeDtypeStruct((groups, GROUP * 4, HALF), jnp.bfloat16),
        ],
        scratch_shapes=[
            pltpu.VMEM((planes, 32, FACE), jnp.bfloat16),
            pltpu.VMEM((FACE, HALF), jnp.bfloat16),
            pltpu.SemaphoreType.DMA((planes // 16 + 1,)),
        ],
        compiler_params=params(),
        cost_estimate=pl.CostEstimate(
            flops=2 * planes * 32 * FACE * HALF,
            bytes_accessed=planes * 32 * (FACE + HALF) * 2,
            transcendentals=0,
        ),
        name="blur_across",
    )(raw, table)


def last_kernel(tile_ref, across_ref, halo_ref, grouped_ref, out_ref):
    last = across_ref.shape[0] - 1
    stacked = jnp.concatenate([across_ref[last], halo_ref[last]], axis=0)
    weights = grouped_ref[jnp.minimum(tile_ref[0], 1), (GROUP - 1) * 16 :]
    out_ref[...] = dot(weights, stacked).astype(jnp.bfloat16)


def last_planar(tile, across, halo, grouped):
    return pl.pallas_call(
        last_kernel,
        in_specs=[whole(pltpu.SMEM)] + [whole()] * 3,
        out_specs=whole(),
        out_shape=jax.ShapeDtypeStruct((16, HALF), jnp.bfloat16),
        compiler_params=params(),
        name="last_planar",
    )(tile, across, halo, grouped)


def blend(before, middle, after):
    total = before.astype(jnp.float32) + 2.0 * middle.astype(jnp.float32)
    return ((total + after.astype(jnp.float32)) * 0.25).astype(jnp.bfloat16)


def section_kernel(
    tile_ref, across_ref, halo_ref, grouped_ref, table_ref, out_ref, head_ref, planar_ref
):
    groups = across_ref.shape[0]
    weights = grouped_ref[jnp.minimum(tile_ref[0], 1)]
    for g in range(groups):
        stacked = jnp.concatenate([across_ref[g], halo_ref[g]], axis=0)
        planar = dot(weights, stacked).astype(jnp.bfloat16)
        planar_ref[g * GROUP : (g + 1) * GROUP] = planar.reshape(GROUP, 16, HALF)
    head_ref[0] = planar_ref[0]
    head_ref[16] = planar_ref[1]
    table = table_ref[...]
    sections = groups * GROUP // 2
    for m in range(sections // 16):
        made = [
            blend(planar_ref[2 * s - 1], planar_ref[2 * s], planar_ref[2 * s + 1])
            for s in range(max(1, m * 16), (m + 1) * 16)
        ]
        if m == 0:
            for k in range(15):
                head_ref[1 + k] = made[k]
            continue
        rows = jnp.concatenate(made, axis=0)
        out_ref[:, m * HALF : (m + 1) * HALF] = dot_nt(table, rows).astype(jnp.bfloat16)


def row_spectra(tile, across, halo, grouped, table):
    planes = across.shape[0] * GROUP
    rows = planes // 2 * 16
    return pl.pallas_call(
        section_kernel,
        in_specs=[whole(pltpu.SMEM)] + [whole()] * 4,
        out_specs=[whole()] * 2,
        out_shape=[
            jax.ShapeDtypeStruct((HALF, rows), jnp.bfloat16),
            jax.ShapeDtypeStruct((17, 16, HALF), jnp.bfloat16),
        ],
        scratch_shapes=[pltpu.VMEM((planes, 16, HALF), jnp.bfloat16)],
        compiler_params=params(),
        cost_estimate=pl.CostEstimate(
            flops=2 * planes * 16 * 288 * HALF,
            bytes_accessed=planes * 32 * HALF * 2,
            transcendentals=0,
        ),
        name="row_spectra",
    )(tile, across, halo, grouped, table)


def head_kernel(
    tile_ref, slab_ref, next_ref, behind_ref, corner_ref, blur_ref, single_ref,
    head_ref, table_ref, spectra_ref, out_ref,
):
    rows = jnp.concatenate([behind_ref[...], corner_ref[24:]], axis=0)
    rows = dot(rows, blur_ref[...]).astype(jnp.bfloat16)
    weights = single_ref[jnp.minimum(tile_ref[0], 1)]
    far = dot(weights, rows)
    wrapped = lax.rem(slab_ref[0], DEPTH) == 0
    before = jnp.where(wrapped, far, next_ref[...].astype(jnp.float32))
    first = blend(before.astype(jnp.bfloat16), head_ref[0], head_ref[16])
    rows = jnp.concatenate([first] + [head_ref[k] for k in range(1, 16)], axis=0)
    out_ref[...] = dot_nt(table_ref[...], rows).astype(jnp.bfloat16)


def head_spectra(tile, slab, near, behind, corner, blur, single, head, table, spectra):
    return pl.pallas_call(
        head_kernel,
        grid=(1,),
        in_specs=[whole(pltpu.SMEM)] * 2 + [whole()] * 7 + [pl.BlockSpec(memory_space=pl.ANY)],
        out_specs=pl.BlockSpec((HALF, HALF), lambda g: (0, 0)),
        out_shape=jax.ShapeDtypeStruct(spectra.shape, jnp.bfloat16),
        input_output_aliases={9: 0},
        compiler_params=params(),
        name="head_spectra",
    )(tile, slab, near, behind, corner, blur, single, head, table, spectra)


def cross_kernel(
    tile_ref, meta_ref, spectra_ref, table_ref, out_ref, held_ref, band_ref
):
    pairs = meta_ref.shape[1]
    blocks = spectra_ref.shape[2] // 128
    lane = lax.broadcasted_iota(jnp.int32, (16, 128), 1)
    out_ref[...] = jnp.zeros_like(out_ref)
    for k in range(blocks):
        for h in range(2):
            a = [
                spectra_ref[8 * h + t, :, 128 * k : 128 * (k + 1)].astype(jnp.float32)
                for t in range(8)
            ]
            for bit in (1, 2, 4):
                low = (lane // 16) & bit == 0
                for i in range(8):
                    if i & bit:
                        continue
                    j = i + bit
                    first = jnp.where(low, a[i], pltpu.roll(a[j], 16 * bit, 1))
                    second = jnp.where(low, pltpu.roll(a[i], 128 - 16 * bit, 1), a[j])
                    a[i], a[j] = first, second
            for s in range(8):
                held_ref[8 * k + s, h] = a[s]

    batch = 8
    steps = pairs // batch
    eight = (FREQS, 128)
    column = lax.broadcasted_iota(jnp.int32, eight, 1)
    special = (lax.broadcasted_iota(jnp.int32, eight, 0) == 0) & (tile_ref[0] == 0)
    upper = column > BAND // 2

    def cut(step, buffer):
        for p in range(batch):
            n = step * batch + p
            live = lane < meta_ref[4, n]
            for side in range(2):
                which = meta_ref[side, n]
                start = meta_ref[2 + side, n]
                from_low = (lane >= start) | (lane < start - 128)
                mixed = jnp.where(from_low, held_ref[which, 0], held_ref[which, 1])
                turned = pltpu.roll(mixed, (256 - start) & 127, 1)
                band = jnp.where(live, turned, 0.0)
                band_ref[buffer, 2 * p + side] = band.astype(jnp.bfloat16)

    def cross(step, buffer):
        bands = band_ref[buffer].reshape(2 * batch * 16, 128)
        full = dot(bands, table_ref[...])
        for p in range(batch):
            real, imag, edge_real, edge_imag = [], [], [], []
            for side in range(2):
                at = (2 * p + side) * 16
                cos_re = full[at : at + 8, :128]
                sin_re = full[at : at + 8, 128:]
                cos_im = full[at + 8 : at + 16, :128]
                sin_im = full[at + 8 : at + 16, 128:]
                real.append(cos_re + jnp.where(special, 0.0, sin_im))
                imag.append(jnp.where(special, 0.0, cos_im) - sin_re)
                edge_real.append(cos_im)
                edge_imag.append(-sin_im)
            cross_real = real[0] * real[1] + imag[0] * imag[1]
            cross_imag = imag[0] * real[1] - real[0] * imag[1]
            last_real = edge_real[0] * edge_real[1] + edge_imag[0] * edge_imag[1]
            last_imag = edge_imag[0] * edge_real[1] - edge_real[0] * edge_imag[1]
            first_slot = jnp.where(special & upper, cross_imag, cross_real)
            packed = jnp.where(upper, last_imag, last_real)
            second_slot = jnp.where(special, packed, cross_imag)
            both = jnp.concatenate([first_slot, second_slot], axis=0)
            out_ref[meta_ref[5, step * batch + p]] = both.astype(jnp.bfloat16)

    cut(0, 0)

    def body(step, _):
        cross(step, step & 1)
        cut(step + 1, (step + 1) & 1)
        return 0

    lax.fori_loop(0, steps - 1, body, 0)
    cross(steps - 1, (steps - 1) & 1)


def pair_table(sections, rows, extents, owners):
    position = jnp.arange(owners.shape[0], dtype=jnp.int32)
    earlier = (owners[:, None] == owners[None, :]) & (position[None, :] < position[:, None])
    slots = jnp.sum(earlier.astype(jnp.int32), axis=1)
    places = owners * OWN_CAP + slots
    return jnp.concatenate([sections.T, rows.T + 1, extents[None], places[None]], axis=0)


def cross_spectra(tile, meta, spectra, table):
    held = spectra.shape[2] // 16
    return pl.pallas_call(
        cross_kernel,
        in_specs=[whole(pltpu.SMEM)] * 2 + [whole()] * 2,
        out_specs=whole(),
        out_shape=jax.ShapeDtypeStruct((TILES * OWN_CAP, 16, 128), jnp.bfloat16),
        scratch_shapes=[
            pltpu.VMEM((held, 2, 16, 128), jnp.float32),
            pltpu.VMEM((2, 16, 16, 128), jnp.bfloat16),
        ],
        compiler_params=params(),
        name="cross_spectra",
    )(tile, meta, spectra, table)


def surface_kernel(
    cross_ref, reversal_ref, column_ref, row_ref, out_hbm, turned_ref, size_ref,
    norm_ref, col_ref, out_ref, sems,
):
    lane = lax.broadcasted_iota(jnp.int32, (FREQS, 128), 1)
    top = lax.broadcasted_iota(jnp.int32, (FREQS, 128), 0) == 0
    edge = lax.broadcasted_iota(jnp.int32, (128, 128), 1) == 0
    upper = lane > BAND // 2
    ends = (lane == 0) | (lane == BAND // 2)

    turned = dot(cross_ref[0].reshape(OWN_CAP * 16, 128), reversal_ref[...])
    turned_ref[...] = turned.reshape(OWN_CAP, 16, 128)

    def unpack(packed, turned):
        real = jnp.where(upper, turned, packed)
        imag = jnp.where(upper, packed, jnp.where(ends, 0.0, -turned))
        return real, imag

    def rounded(value):
        return value.astype(jnp.bfloat16).astype(jnp.float32)

    def replaced(row, rows):
        return jnp.concatenate([jnp.where(top, row, rows[:8]), rows[8:]], axis=0)

    def parts(slot):
        block = cross_ref[:, slot].astype(jnp.float32)
        real = block[:, :8, :].reshape(128, 128)
        imag = block[:, 8:, :].reshape(128, 128)
        turned = turned_ref[slot]
        real_0, imag_0 = unpack(real[:8], turned[:8])
        real_n, imag_n = unpack(imag[:8], turned[8:])
        return replaced(real_0, real), replaced(imag_0, imag), real_n, imag_n

    def magnitude(real, imag):
        power = real * real + imag * imag
        return power * lax.rsqrt(jnp.maximum(power, 1e-30))

    means = []
    for slot in range(OWN_CAP):
        real, imag, real_n, imag_n = parts(slot)
        size = magnitude(real, imag)
        size_n = magnitude(real_n, imag_n)
        size_ref[slot, :128] = size
        size_ref[slot, 128:] = size_n
        total = 2.0 * jnp.sum(size.reshape(16, 8, 128), axis=0)
        total = jnp.sum(total + jnp.where(top, size_n - size[:8], 0.0))
        means.append(total / (BAND * HALF) + 1e-06)
    for slot in range(OWN_CAP):
        real, imag, real_n, imag_n = parts(slot)
        scale = 1.0 / (size_ref[slot, :128] + means[slot])
        scale_n = 1.0 / (size_ref[slot, 128:] + means[slot])
        norm_real = real * scale
        norm_imag = imag * scale
        zero = rounded(norm_real[:8]) - rounded(norm_imag[:8])
        last = rounded(real_n * scale_n) - rounded(imag_n * scale_n)
        norm_ref[slot, :128] = replaced(zero, norm_real).astype(jnp.bfloat16)
        norm_ref[slot, 128:] = replaced(last, norm_imag).astype(jnp.bfloat16)
    for slot in range(OWN_CAP):
        full = dot_nt(column_ref[...], norm_ref[slot])
        cos_re, cos_im = full[:128, :128], full[:128, 128:]
        sin_re, sin_im = full[128:, :128], full[128:, 128:]
        col_real = cos_re + jnp.where(edge, sin_re, -sin_im)
        col_imag = cos_im + jnp.where(edge, sin_im, sin_re)
        col_ref[slot, :, :128] = col_real.astype(jnp.bfloat16)
        col_ref[slot, :, 128:] = col_imag.astype(jnp.bfloat16)
    step = 3
    copies = []
    for k in range(OWN_CAP // step):
        held = slice(k * step, (k + 1) * step)
        made = dot(col_ref[held].reshape(step * BAND, HALF), row_ref[...])
        out_ref[held] = made.astype(jnp.bfloat16).reshape(step, BAND, HALF)
        held = pl.ds(k * step, step)
        copies.append(
            pltpu.make_async_copy(out_ref.at[held], out_hbm.at[held], sems.at[k])
        )
        copies[-1].start()
    for copy in copies:
        copy.wait()


def surfaces(cross, back, column, row):
    return pl.pallas_call(
        surface_kernel,
        in_specs=[whole()] * 4,
        out_specs=whole(pltpu.HBM),
        out_shape=jax.ShapeDtypeStruct((OWN_CAP, BAND, HALF), jnp.bfloat16),
        scratch_shapes=[
            pltpu.VMEM((OWN_CAP, 16, 128), jnp.float32),
            pltpu.VMEM((OWN_CAP, 136, 128), jnp.float32),
            pltpu.VMEM((OWN_CAP, HALF, 128), jnp.bfloat16),
            pltpu.VMEM((OWN_CAP, BAND, HALF), jnp.bfloat16),
            pltpu.VMEM((OWN_CAP, BAND, HALF), jnp.bfloat16),
            pltpu.SemaphoreType.DMA((4,)),
        ],
        compiler_params=params(),
        name="surfaces",
    )(cross, back, column, row)


def correlate(raw_planes, pair_sections, pair_rows, pair_extent, pair_owner):
    tile = lax.axis_index("tile").astype(jnp.int32).reshape(1)
    slab = lax.axis_index("plane").astype(jnp.int32).reshape(1)
    slabs = lax.axis_size("plane")
    planes = raw_planes.shape[0]
    owners = pair_owner[:, 0]

    far = [s for s in range(slabs - 1) if (s + 1) % DEPTH == 0]
    near = [s for s in range(slabs - 1) if (s + 1) % DEPTH]
    turns = [(t, (t + 1) % TILES) for t in range(TILES)]
    corners = [(s * TILES + t, (s + 1) * TILES + u) for s in far for t, u in turns]
    last = raw_planes[planes - 1]
    behind = lax.ppermute(last, "plane", [(s, s + 1) for s in far])
    corner = lax.ppermute(last, ("plane", "tile"), corners)
    table = pltpu.with_memory_space_constraint(jnp.asarray(blur_matrix()), pltpu.HBM)
    held = pltpu.with_memory_space_constraint(raw_planes, pltpu.HBM)
    across, edges = blur_across(held, table)
    halo = lax.ppermute(edges, "tile", turns)
    grouped, single = column_tables()
    meta = pair_table(pair_sections, pair_rows, pair_extent, owners)
    last = last_planar(tile, across, halo, grouped)
    last = lax.ppermute(last, "plane", [(s, s + 1) for s in near])
    spectra, head = row_spectra(tile, across, halo, grouped, row_transform_table())
    spectra = head_spectra(
        tile, slab, last, behind, corner, blur_matrix(), single, head,
        row_transform_table(), spectra,
    )
    spectra, meta = lax.optimization_barrier((spectra, meta))
    spectra = lax.all_to_all(
        spectra.reshape(TILES, 16, spectra.shape[1]), "tile", 0, 0, tiled=True
    )

    cos_band, sin_band = dft_tables(BAND)
    cross = cross_spectra(
        tile, meta, spectra, np.concatenate([cos_band, sin_band], axis=1)
    )
    cross = lax.all_to_all(
        cross.reshape(TILES, OWN_CAP * 16, 128), "tile", 0, 0, tiled=True
    )
    return surfaces(
        cross.reshape(TILES, OWN_CAP, 16, 128),
        reversal(),
        np.concatenate([cos_band, sin_band], axis=0),
        row_inverse_table(),
    )


def solution(mesh):
    return jax.shard_map(
        correlate,
        mesh=mesh,
        in_specs=(
            P("plane", "tile", None),
            P("plane", None),
            P("plane", None),
            P("plane"),
            P("plane", None),
        ),
        out_specs=P(("plane", "tile"), None, None),
        check_vma=False,
    )
```

```python
import math

import jax
import jax.numpy as jnp
import numpy as np
from jax import lax
from jax.experimental import pallas as pl
from jax.experimental.pallas import tpu as pltpu
from jax.sharding import PartitionSpec as P

BAND = 128
OWN_CAP = 12
FACE = 512
HALF = 256
TILES = 16
DEPTH = 8
FREQS = 8
GROUP = 8
VMEM_LIMIT = 24 * 1024 * 1024


def whole(space=pltpu.VMEM):
    return pl.BlockSpec(memory_space=space)


def params(**kw):
    return pltpu.CompilerParams(vmem_limit_bytes=VMEM_LIMIT, **kw)


def blur_weight(offset):
    offset = abs(offset)
    return (6.0, 4.0, 1.0)[offset] / 16.0 if offset <= 2 else 0.0


def blur_matrix():
    table = np.zeros((FACE, HALF), np.float32)
    for c in range(FACE):
        for j in range(HALF):
            if abs(c - 2 * j) <= 2:
                table[c, j] = blur_weight(c - 2 * j)
    return table.astype(jnp.bfloat16)


def dft_tables(length):
    indices = np.arange(length)
    phases = indices[:, None] * indices[None, :] % length
    angles = phases.astype(np.float32) * np.float32(2.0 * math.pi / length)
    factor = np.float32(1.0 / math.sqrt(length))
    return (
        (np.cos(angles) * factor).astype(jnp.bfloat16),
        (np.sin(angles) * factor).astype(jnp.bfloat16),
    )


def column_weights(first_tile):
    local = np.zeros((16, 32), np.float32)
    halo = np.zeros((16, 4), np.float32)
    for i in range(16):
        for c in range(32):
            local[i, c] = blur_weight(c + 2 - 2 * i)
        for h in range(4):
            halo[i, h] = blur_weight(h - 2 - 2 * i)
    if first_tile:
        local[0, 0] = 0.0
        halo[1, :] = 0.0
    return local, halo


def column_tables():
    grouped = np.zeros((2, GROUP * 16, GROUP * 36), np.float32)
    single = np.zeros((2, 16, 40), np.float32)
    for variant in (0, 1):
        local, halo = column_weights(variant == 0)
        for q in range(GROUP):
            rows = slice(q * 16, q * 16 + 16)
            grouped[variant, rows, q * 32 : q * 32 + 32] = local
            at = GROUP * 32 + q * 4
            grouped[variant, rows, at : at + 4] = halo
        single[variant, :, :32] = local
        single[variant, :, 36:40] = halo
    return grouped.astype(jnp.bfloat16), single.astype(jnp.bfloat16)


def row_transform_table():
    cos_half, sin_half = dft_tables(HALF)
    table = np.zeros((HALF, HALF), np.float32)
    for d in range(TILES):
        for f in range(FREQS):
            v = d * FREQS + f
            table[d * 16 + f] = cos_half[v]
            if v:
                table[d * 16 + FREQS + f] = -sin_half[v].astype(np.float32)
            else:
                table[d * 16 + FREQS + f] = cos_half[HALF // 2]
    return table.astype(jnp.bfloat16)


def row_inverse_table():
    cos_half, sin_half = dft_tables(HALF)
    table = np.zeros((HALF, HALF), np.float32)
    for v in range(HALF // 2):
        table[v] = cos_half[v].astype(np.float32) * (2.0 if v else 1.0)
        if v:
            table[HALF // 2 + v] = sin_half[v].astype(np.float32) * -2.0
        else:
            table[HALF // 2] = cos_half[HALF // 2]
    return table.astype(jnp.bfloat16)


def reversal():
    table = np.zeros((BAND, BAND), np.float32)
    for u in range(BAND):
        table[(BAND - u) % BAND, u] = 1.0
    return table.astype(jnp.bfloat16)


def dot(a, b):
    return jnp.dot(a, b, preferred_element_type=jnp.float32)


def dot_nt(a, b):
    return lax.dot_general(
        a, b, (((1,), (1,)), ((), ())), preferred_element_type=jnp.float32
    )


def edge_kernel(raw_ref, table_hbm, edge_ref, last_ref, strip_ref, table_ref, sems):
    planes = raw_ref.shape[0]
    part = 32
    copies = []
    for k in range(planes // part):
        held = pl.ds(k * part, part)
        copies.append(
            pltpu.make_async_copy(
                raw_ref.at[held, pl.ds(24, 8), :], strip_ref.at[held], sems.at[k]
            )
        )
    copies.insert(1, pltpu.make_async_copy(table_hbm, table_ref, sems.at[planes // part]))
    copies.append(
        pltpu.make_async_copy(raw_ref.at[planes - 1], last_ref, sems.at[planes // part + 1])
    )
    for copy in copies:
        copy.start()
    upper = lax.broadcasted_iota(jnp.int32, (8, HALF), 0) < 4
    per = part // GROUP
    copies.pop(1).wait()
    for k in range(planes // part):
        copies[k].wait()
        cells = strip_ref[k * part : (k + 1) * part].reshape(part * 8, FACE)
        across = dot(cells, table_ref[...])
        edges = []
        for q in range(0, part * 8, 16):
            turned = pltpu.roll(across[q : q + 8], 4, 0)
            edges.append(jnp.where(upper, turned, across[q + 8 : q + 16]))
        edges = jnp.concatenate(edges, axis=0).astype(jnp.bfloat16)
        edge_ref[k * per : (k + 1) * per] = edges.reshape(per, GROUP * 4, HALF)
    copies[-1].wait()


def blur_edges(raw, table):
    planes = raw.shape[0]
    return pl.pallas_call(
        edge_kernel,
        in_specs=[whole(pltpu.HBM)] * 2,
        out_specs=[whole()] * 2,
        out_shape=[
            jax.ShapeDtypeStruct((planes // GROUP, GROUP * 4, HALF), jnp.bfloat16),
            jax.ShapeDtypeStruct((32, FACE), jnp.bfloat16),
        ],
        scratch_shapes=[
            pltpu.VMEM((planes, 8, FACE), jnp.bfloat16),
            pltpu.VMEM((FACE, HALF), jnp.bfloat16),
            pltpu.SemaphoreType.DMA((planes // 32 + 2,)),
        ],
        compiler_params=params(),
        cost_estimate=pl.CostEstimate(
            flops=2 * planes * 8 * FACE * HALF,
            bytes_accessed=planes * 8 * FACE * 2,
            transcendentals=0,
        ),
        name="blur_edges",
    )(raw, table)


def across_kernel(raw_ref, table_ref, across_ref):
    planes = raw_ref.shape[0]
    part = 16
    per = part // GROUP
    for k in range(planes // part):
        cells = raw_ref[k * part : (k + 1) * part].reshape(part * 32, FACE)
        across = dot(cells, table_ref[...]).astype(jnp.bfloat16)
        across_ref[k * per : (k + 1) * per] = across.reshape(per, GROUP * 32, HALF)


def blur_across(raw, table):
    planes = raw.shape[0]
    return pl.pallas_call(
        across_kernel,
        in_specs=[whole()] * 2,
        out_specs=whole(),
        out_shape=jax.ShapeDtypeStruct((planes // GROUP, GROUP * 32, HALF), jnp.bfloat16),
        compiler_params=params(),
        cost_estimate=pl.CostEstimate(
            flops=2 * planes * 32 * FACE * HALF,
            bytes_accessed=planes * 32 * (FACE + HALF) * 2,
            transcendentals=0,
        ),
        name="blur_across",
    )(raw, table)


def last_kernel(tile_ref, across_ref, halo_ref, grouped_ref, out_ref):
    last = across_ref.shape[0] - 1
    stacked = jnp.concatenate([across_ref[last], halo_ref[last]], axis=0)
    weights = grouped_ref[jnp.minimum(tile_ref[0], 1), (GROUP - 1) * 16 :]
    out_ref[...] = dot(weights, stacked).astype(jnp.bfloat16)


def last_planar(tile, across, halo, grouped):
    return pl.pallas_call(
        last_kernel,
        in_specs=[whole(pltpu.SMEM)] + [whole()] * 3,
        out_specs=whole(),
        out_shape=jax.ShapeDtypeStruct((16, HALF), jnp.bfloat16),
        compiler_params=params(),
        name="last_planar",
    )(tile, across, halo, grouped)


def blend(before, middle, after):
    total = before.astype(jnp.float32) + 2.0 * middle.astype(jnp.float32)
    return ((total + after.astype(jnp.float32)) * 0.25).astype(jnp.bfloat16)


def section_kernel(
    tile_ref, across_ref, halo_ref, grouped_ref, table_ref, out_ref, head_ref, planar_ref
):
    groups = across_ref.shape[0]
    weights = grouped_ref[jnp.minimum(tile_ref[0], 1)]
    for g in range(groups):
        stacked = jnp.concatenate([across_ref[g], halo_ref[g]], axis=0)
        planar = dot(weights, stacked).astype(jnp.bfloat16)
        planar_ref[g * GROUP : (g + 1) * GROUP] = planar.reshape(GROUP, 16, HALF)
    head_ref[0] = planar_ref[0]
    head_ref[16] = planar_ref[1]
    table = table_ref[...]
    sections = groups * GROUP // 2
    for m in range(sections // 16):
        made = [
            blend(planar_ref[2 * s - 1], planar_ref[2 * s], planar_ref[2 * s + 1])
            for s in range(max(1, m * 16), (m + 1) * 16)
        ]
        if m == 0:
            for k in range(15):
                head_ref[1 + k] = made[k]
            continue
        rows = jnp.concatenate(made, axis=0)
        out_ref[:, m * HALF : (m + 1) * HALF] = dot_nt(table, rows).astype(jnp.bfloat16)


def row_spectra(tile, across, halo, grouped, table):
    planes = across.shape[0] * GROUP
    rows = planes // 2 * 16
    return pl.pallas_call(
        section_kernel,
        in_specs=[whole(pltpu.SMEM)] + [whole()] * 4,
        out_specs=[whole()] * 2,
        out_shape=[
            jax.ShapeDtypeStruct((HALF, rows), jnp.bfloat16),
            jax.ShapeDtypeStruct((17, 16, HALF), jnp.bfloat16),
        ],
        scratch_shapes=[pltpu.VMEM((planes, 16, HALF), jnp.bfloat16)],
        compiler_params=params(),
        cost_estimate=pl.CostEstimate(
            flops=2 * planes * 16 * 288 * HALF,
            bytes_accessed=planes * 32 * HALF * 2,
            transcendentals=0,
        ),
        name="row_spectra",
    )(tile, across, halo, grouped, table)


def head_kernel(
    tile_ref, slab_ref, next_ref, behind_ref, corner_ref, blur_ref, single_ref,
    head_ref, table_ref, spectra_ref, out_ref,
):
    rows = jnp.concatenate([behind_ref[...], corner_ref[24:]], axis=0)
    rows = dot(rows, blur_ref[...]).astype(jnp.bfloat16)
    weights = single_ref[jnp.minimum(tile_ref[0], 1)]
    far = dot(weights, rows)
    wrapped = lax.rem(slab_ref[0], DEPTH) == 0
    before = jnp.where(wrapped, far, next_ref[...].astype(jnp.float32))
    first = blend(before.astype(jnp.bfloat16), head_ref[0], head_ref[16])
    rows = jnp.concatenate([first] + [head_ref[k] for k in range(1, 16)], axis=0)
    out_ref[...] = dot_nt(table_ref[...], rows).astype(jnp.bfloat16)


def head_spectra(tile, slab, near, behind, corner, blur, single, head, table, spectra):
    return pl.pallas_call(
        head_kernel,
        grid=(1,),
        in_specs=[whole(pltpu.SMEM)] * 2 + [whole()] * 7 + [pl.BlockSpec(memory_space=pl.ANY)],
        out_specs=pl.BlockSpec((HALF, HALF), lambda g: (0, 0)),
        out_shape=jax.ShapeDtypeStruct(spectra.shape, jnp.bfloat16),
        input_output_aliases={9: 0},
        compiler_params=params(),
        name="head_spectra",
    )(tile, slab, near, behind, corner, blur, single, head, table, spectra)


def cross_kernel(
    tile_ref, meta_ref, spectra_ref, table_ref, out_ref, held_ref, band_ref
):
    pairs = meta_ref.shape[1]
    blocks = spectra_ref.shape[2] // 128
    lane = lax.broadcasted_iota(jnp.int32, (16, 128), 1)
    out_ref[...] = jnp.zeros_like(out_ref)
    for k in range(blocks):
        for h in range(2):
            a = [
                spectra_ref[8 * h + t, :, 128 * k : 128 * (k + 1)].astype(jnp.float32)
                for t in range(8)
            ]
            for bit in (1, 2, 4):
                low = (lane // 16) & bit == 0
                for i in range(8):
                    if i & bit:
                        continue
                    j = i + bit
                    first = jnp.where(low, a[i], pltpu.roll(a[j], 16 * bit, 1))
                    second = jnp.where(low, pltpu.roll(a[i], 128 - 16 * bit, 1), a[j])
                    a[i], a[j] = first, second
            for s in range(8):
                held_ref[8 * k + s, h] = a[s]

    batch = 32
    steps = pairs // batch
    eight = (FREQS, 128)
    column = lax.broadcasted_iota(jnp.int32, eight, 1)
    special = (lax.broadcasted_iota(jnp.int32, eight, 0) == 0) & (tile_ref[0] == 0)
    upper = column > BAND // 2

    def cut(step, buffer):
        for p in range(batch):
            n = step * batch + p
            live = lane < meta_ref[4, n]
            for side in range(2):
                which = meta_ref[side, n]
                start = meta_ref[2 + side, n]
                from_low = (lane >= start) | (lane < start - 128)
                mixed = jnp.where(from_low, held_ref[which, 0], held_ref[which, 1])
                turned = pltpu.roll(mixed, (256 - start) & 127, 1)
                band = jnp.where(live, turned, 0.0)
                band_ref[buffer, 2 * p + side] = band.astype(jnp.bfloat16)

    def cross(step, buffer):
        bands = band_ref[buffer].reshape(2 * batch * 16, 128)
        full = dot(bands, table_ref[...])
        for p in range(batch):
            real, imag, edge_real, edge_imag = [], [], [], []
            for side in range(2):
                at = (2 * p + side) * 16
                cos_re = full[at : at + 8, :128]
                sin_re = full[at : at + 8, 128:]
                cos_im = full[at + 8 : at + 16, :128]
                sin_im = full[at + 8 : at + 16, 128:]
                real.append(cos_re + jnp.where(special, 0.0, sin_im))
                imag.append(jnp.where(special, 0.0, cos_im) - sin_re)
                edge_real.append(cos_im)
                edge_imag.append(-sin_im)
            cross_real = real[0] * real[1] + imag[0] * imag[1]
            cross_imag = imag[0] * real[1] - real[0] * imag[1]
            last_real = edge_real[0] * edge_real[1] + edge_imag[0] * edge_imag[1]
            last_imag = edge_imag[0] * edge_real[1] - edge_real[0] * edge_imag[1]
            first_slot = jnp.where(special & upper, cross_imag, cross_real)
            packed = jnp.where(upper, last_imag, last_real)
            second_slot = jnp.where(special, packed, cross_imag)
            both = jnp.concatenate([first_slot, second_slot], axis=0)
            out_ref[meta_ref[5, step * batch + p]] = both.astype(jnp.bfloat16)

    cut(0, 0)

    def body(step, _):
        cross(step, step & 1)
        cut(step + 1, (step + 1) & 1)
        return 0

    lax.fori_loop(0, steps - 1, body, 0)
    cross(steps - 1, (steps - 1) & 1)


def pair_table(sections, rows, extents, owners):
    position = jnp.arange(owners.shape[0], dtype=jnp.int32)
    earlier = (owners[:, None] == owners[None, :]) & (position[None, :] < position[:, None])
    slots = jnp.sum(earlier.astype(jnp.int32), axis=1)
    places = owners * OWN_CAP + slots
    return jnp.concatenate([sections.T, rows.T + 1, extents[None], places[None]], axis=0)


def cross_spectra(tile, meta, spectra, table):
    held = spectra.shape[2] // 16
    return pl.pallas_call(
        cross_kernel,
        in_specs=[whole(pltpu.SMEM)] * 2 + [whole()] * 2,
        out_specs=whole(),
        out_shape=jax.ShapeDtypeStruct((TILES * OWN_CAP, 16, 128), jnp.bfloat16),
        scratch_shapes=[
            pltpu.VMEM((held, 2, 16, 128), jnp.float32),
            pltpu.VMEM((2, 64, 16, 128), jnp.bfloat16),
        ],
        compiler_params=params(),
        name="cross_spectra",
    )(tile, meta, spectra, table)


def surface_kernel(
    cross_ref, reversal_ref, column_ref, row_ref, out_hbm, turned_ref, size_ref,
    norm_ref, col_ref, out_ref, sems,
):
    lane = lax.broadcasted_iota(jnp.int32, (FREQS, 128), 1)
    top = lax.broadcasted_iota(jnp.int32, (FREQS, 128), 0) == 0
    edge = lax.broadcasted_iota(jnp.int32, (128, 128), 1) == 0
    upper = lane > BAND // 2
    ends = (lane == 0) | (lane == BAND // 2)

    turned = dot(cross_ref[0].reshape(OWN_CAP * 16, 128), reversal_ref[...])
    turned_ref[...] = turned.reshape(OWN_CAP, 16, 128)

    def unpack(packed, turned):
        real = jnp.where(upper, turned, packed)
        imag = jnp.where(upper, packed, jnp.where(ends, 0.0, -turned))
        return real, imag

    def rounded(value):
        return value.astype(jnp.bfloat16).astype(jnp.float32)

    def replaced(row, rows):
        return jnp.concatenate([jnp.where(top, row, rows[:8]), rows[8:]], axis=0)

    def parts(slot):
        block = cross_ref[:, slot].astype(jnp.float32)
        real = block[:, :8, :].reshape(128, 128)
        imag = block[:, 8:, :].reshape(128, 128)
        turned = turned_ref[slot]
        real_0, imag_0 = unpack(real[:8], turned[:8])
        real_n, imag_n = unpack(imag[:8], turned[8:])
        return replaced(real_0, real), replaced(imag_0, imag), real_n, imag_n

    def magnitude(real, imag):
        power = real * real + imag * imag
        return power * lax.rsqrt(jnp.maximum(power, 1e-30))

    means = []
    for slot in range(OWN_CAP):
        real, imag, real_n, imag_n = parts(slot)
        size = magnitude(real, imag)
        size_n = magnitude(real_n, imag_n)
        size_ref[slot, :128] = size
        size_ref[slot, 128:] = size_n
        total = 2.0 * jnp.sum(size.reshape(16, 8, 128), axis=0)
        total = jnp.sum(total + jnp.where(top, size_n - size[:8], 0.0))
        means.append(total / (BAND * HALF) + 1e-06)
    for slot in range(OWN_CAP):
        real, imag, real_n, imag_n = parts(slot)
        scale = 1.0 / (size_ref[slot, :128] + means[slot])
        scale_n = 1.0 / (size_ref[slot, 128:] + means[slot])
        norm_real = real * scale
        norm_imag = imag * scale
        zero = rounded(norm_real[:8]) - rounded(norm_imag[:8])
        last = rounded(real_n * scale_n) - rounded(imag_n * scale_n)
        norm_ref[slot, :128] = replaced(zero, norm_real).astype(jnp.bfloat16)
        norm_ref[slot, 128:] = replaced(last, norm_imag).astype(jnp.bfloat16)
    for slot in range(OWN_CAP):
        full = dot_nt(column_ref[...], norm_ref[slot])
        cos_re, cos_im = full[:128, :128], full[:128, 128:]
        sin_re, sin_im = full[128:, :128], full[128:, 128:]
        col_real = cos_re + jnp.where(edge, sin_re, -sin_im)
        col_imag = cos_im + jnp.where(edge, sin_im, sin_re)
        col_ref[slot, :, :128] = col_real.astype(jnp.bfloat16)
        col_ref[slot, :, 128:] = col_imag.astype(jnp.bfloat16)
    step = 3
    copies = []
    for k in range(OWN_CAP // step):
        held = slice(k * step, (k + 1) * step)
        made = dot(col_ref[held].reshape(step * BAND, HALF), row_ref[...])
        out_ref[held] = made.astype(jnp.bfloat16).reshape(step, BAND, HALF)
        held = pl.ds(k * step, step)
        copies.append(
            pltpu.make_async_copy(out_ref.at[held], out_hbm.at[held], sems.at[k])
        )
        copies[-1].start()
    for copy in copies:
        copy.wait()


def surfaces(cross, back, column, row):
    return pl.pallas_call(
        surface_kernel,
        in_specs=[whole()] * 4,
        out_specs=whole(pltpu.HBM),
        out_shape=jax.ShapeDtypeStruct((OWN_CAP, BAND, HALF), jnp.bfloat16),
        scratch_shapes=[
            pltpu.VMEM((OWN_CAP, 16, 128), jnp.float32),
            pltpu.VMEM((OWN_CAP, 136, 128), jnp.float32),
            pltpu.VMEM((OWN_CAP, HALF, 128), jnp.bfloat16),
            pltpu.VMEM((OWN_CAP, BAND, HALF), jnp.bfloat16),
            pltpu.VMEM((OWN_CAP, BAND, HALF), jnp.bfloat16),
            pltpu.SemaphoreType.DMA((4,)),
        ],
        compiler_params=params(),
        name="surfaces",
    )(cross, back, column, row)


def correlate(raw_planes, pair_sections, pair_rows, pair_extent, pair_owner):
    tile = lax.axis_index("tile").astype(jnp.int32).reshape(1)
    slab = lax.axis_index("plane").astype(jnp.int32).reshape(1)
    slabs = lax.axis_size("plane")
    owners = pair_owner[:, 0]

    far = [s for s in range(slabs - 1) if (s + 1) % DEPTH == 0]
    near = [s for s in range(slabs - 1) if (s + 1) % DEPTH]
    turns = [(t, (t + 1) % TILES) for t in range(TILES)]
    corners = [(s * TILES + t, (s + 1) * TILES + u) for s in far for t, u in turns]
    table = pltpu.with_memory_space_constraint(jnp.asarray(blur_matrix()), pltpu.HBM)
    held = pltpu.with_memory_space_constraint(raw_planes, pltpu.HBM)
    edges, last = blur_edges(held, table)
    halo = lax.ppermute(edges, "tile", turns)
    behind = lax.ppermute(last, "plane", [(s, s + 1) for s in far])
    corner = lax.ppermute(last, ("plane", "tile"), corners)
    across = blur_across(raw_planes, blur_matrix())
    grouped, single = column_tables()
    meta = pair_table(pair_sections, pair_rows, pair_extent, owners)
    last = last_planar(tile, across, halo, grouped)
    last = lax.ppermute(last, "plane", [(s, s + 1) for s in near])
    spectra, head = row_spectra(tile, across, halo, grouped, row_transform_table())
    spectra = head_spectra(
        tile, slab, last, behind, corner, blur_matrix(), single, head,
        row_transform_table(), spectra,
    )
    spectra, meta = lax.optimization_barrier((spectra, meta))
    spectra = lax.all_to_all(
        spectra.reshape(TILES, 16, spectra.shape[1]), "tile", 0, 0, tiled=True
    )

    cos_band, sin_band = dft_tables(BAND)
    cross = cross_spectra(
        tile, meta, spectra, np.concatenate([cos_band, sin_band], axis=1)
    )
    cross = lax.all_to_all(
        cross.reshape(TILES, OWN_CAP * 16, 128), "tile", 0, 0, tiled=True
    )
    return surfaces(
        cross.reshape(TILES, OWN_CAP, 16, 128),
        reversal(),
        np.concatenate([cos_band, sin_band], axis=0),
        row_inverse_table(),
    )


def solution(mesh):
    return jax.shard_map(
        correlate,
        mesh=mesh,
        in_specs=(
            P("plane", "tile", None),
            P("plane", None),
            P("plane", None),
            P("plane"),
            P("plane", None),
        ),
        out_specs=P(("plane", "tile"), None, None),
        check_vma=False,
    )
```

```python
import math

import jax
import jax.numpy as jnp
import numpy as np
from jax import lax
from jax.experimental import pallas as pl
from jax.experimental.pallas import tpu as pltpu
from jax.sharding import PartitionSpec as P

BAND = 128
OWN_CAP = 12
FACE = 512
HALF = 256
TILES = 16
DEPTH = 8
HALO = 3
FREQS = 8
GROUP = 8
VMEM_LIMIT = 24 * 1024 * 1024


def whole(space=pltpu.VMEM):
    return pl.BlockSpec(memory_space=space)


def params(**kw):
    return pltpu.CompilerParams(vmem_limit_bytes=VMEM_LIMIT, **kw)


def blur_weight(offset):
    offset = abs(offset)
    return (6.0, 4.0, 1.0)[offset] / 16.0 if offset <= 2 else 0.0


def blur_matrix():
    table = np.zeros((FACE, HALF), np.float32)
    for c in range(FACE):
        for j in range(HALF):
            if abs(c - 2 * j) <= 2:
                table[c, j] = blur_weight(c - 2 * j)
    return table.astype(jnp.bfloat16)


def dft_tables(length):
    indices = np.arange(length)
    phases = indices[:, None] * indices[None, :] % length
    angles = phases.astype(np.float32) * np.float32(2.0 * math.pi / length)
    factor = np.float32(1.0 / math.sqrt(length))
    return (
        (np.cos(angles) * factor).astype(jnp.bfloat16),
        (np.sin(angles) * factor).astype(jnp.bfloat16),
    )


def column_weights(last_tile):
    local = np.zeros((16, 32), np.float32)
    halo = np.zeros((16, HALO), np.float32)
    for i in range(16):
        for c in range(32):
            local[i, c] = blur_weight(c - 2 - 2 * i)
        for h in range(HALO):
            halo[i, h] = blur_weight(30 + h - 2 * i)
    if last_tile:
        halo[14, :] = 0.0
        local[15, :] = 0.0
    return local, halo


def column_tables():
    width = 32 + HALO
    grouped = np.zeros((2, GROUP * 16, GROUP * width), np.float32)
    single = np.zeros((2, 16, 40), np.float32)
    for variant in (0, 1):
        local, halo = column_weights(variant == 1)
        for q in range(GROUP):
            rows = slice(q * 16, q * 16 + 16)
            grouped[variant, rows, q * 32 : q * 32 + 32] = local
            at = GROUP * 32 + q * HALO
            grouped[variant, rows, at : at + HALO] = halo
        single[variant, :, :32] = local
        single[variant, :, 32 : 32 + HALO] = halo
    return grouped.astype(jnp.bfloat16), single.astype(jnp.bfloat16)


def row_transform_table():
    cos_half, sin_half = dft_tables(HALF)
    table = np.zeros((HALF, HALF), np.float32)
    for d in range(TILES):
        for f in range(FREQS):
            v = d * FREQS + f
            table[d * 16 + f] = cos_half[v]
            if v:
                table[d * 16 + FREQS + f] = -sin_half[v].astype(np.float32)
            else:
                table[d * 16 + FREQS + f] = cos_half[HALF // 2]
    return table.astype(jnp.bfloat16)


def row_inverse_table():
    cos_half, sin_half = dft_tables(HALF)
    table = np.zeros((HALF, HALF), np.float32)
    for v in range(HALF // 2):
        table[v] = cos_half[v].astype(np.float32) * (2.0 if v else 1.0)
        if v:
            table[HALF // 2 + v] = sin_half[v].astype(np.float32) * -2.0
        else:
            table[HALF // 2] = cos_half[HALF // 2]
    return table.astype(jnp.bfloat16)


def reversal():
    table = np.zeros((BAND, BAND), np.float32)
    for u in range(BAND):
        table[(BAND - u) % BAND, u] = 1.0
    return table.astype(jnp.bfloat16)


def dot(a, b):
    return jnp.dot(a, b, preferred_element_type=jnp.float32)


def dot_nt(a, b):
    return lax.dot_general(
        a, b, (((1,), (1,)), ((), ())), preferred_element_type=jnp.float32
    )


def edge_kernel(raw_ref, table_hbm, edge_ref, strip_ref, table_ref, sems):
    planes = raw_ref.shape[0]
    part = 32
    copies = []
    for k in range(planes // part):
        held = pl.ds(k * part, part)
        copies.append(
            pltpu.make_async_copy(
                raw_ref.at[held, pl.ds(0, 8), :], strip_ref.at[held], sems.at[k]
            )
        )
    copies.insert(1, pltpu.make_async_copy(table_hbm, table_ref, sems.at[planes // part]))
    for copy in copies:
        copy.start()
    shape = (part * HALO, part * 8)
    row = lax.broadcasted_iota(jnp.int32, shape, 0)
    source = lax.broadcasted_iota(jnp.int32, shape, 1)
    wanted = (source >> 3) * HALO + (source & 7)
    select = jnp.where((row == wanted) & ((source & 7) < HALO), 1.0, 0.0)
    select = select.astype(jnp.bfloat16)
    per = part // GROUP
    copies.pop(1).wait()
    for k in range(planes // part):
        copies[k].wait()
        cells = strip_ref[k * part : (k + 1) * part].reshape(part * 8, FACE)
        across = dot(cells, table_ref[...]).astype(jnp.bfloat16)
        edges = dot(select, across).astype(jnp.bfloat16)
        edge_ref[k * per : (k + 1) * per] = edges.reshape(per, GROUP * HALO, HALF)


def blur_edges(raw, table):
    planes = raw.shape[0]
    return pl.pallas_call(
        edge_kernel,
        in_specs=[whole(pltpu.HBM)] * 2,
        out_specs=whole(),
        out_shape=jax.ShapeDtypeStruct(
            (planes // GROUP, GROUP * HALO, HALF), jnp.bfloat16
        ),
        scratch_shapes=[
            pltpu.VMEM((planes, 8, FACE), jnp.bfloat16),
            pltpu.VMEM((FACE, HALF), jnp.bfloat16),
            pltpu.SemaphoreType.DMA((planes // 32 + 1,)),
        ],
        compiler_params=params(),
        cost_estimate=pl.CostEstimate(
            flops=2 * planes * 8 * FACE * HALF,
            bytes_accessed=planes * 8 * FACE * 2,
            transcendentals=0,
        ),
        name="blur_edges",
    )(raw, table)


def across_kernel(raw_ref, table_ref, across_ref):
    planes = raw_ref.shape[0]
    part = 16
    per = part // GROUP
    for k in range(planes // part):
        cells = raw_ref[k * part : (k + 1) * part].reshape(part * 32, FACE)
        across = dot(cells, table_ref[...]).astype(jnp.bfloat16)
        across_ref[k * per : (k + 1) * per] = across.reshape(per, GROUP * 32, HALF)


def blur_across(raw, table):
    planes = raw.shape[0]
    return pl.pallas_call(
        across_kernel,
        in_specs=[whole()] * 2,
        out_specs=whole(),
        out_shape=jax.ShapeDtypeStruct((planes // GROUP, GROUP * 32, HALF), jnp.bfloat16),
        compiler_params=params(),
        cost_estimate=pl.CostEstimate(
            flops=2 * planes * 32 * FACE * HALF,
            bytes_accessed=planes * 32 * (FACE + HALF) * 2,
            transcendentals=0,
        ),
        name="blur_across",
    )(raw, table)


def last_kernel(tile_ref, across_ref, halo_ref, grouped_ref, out_ref):
    last = across_ref.shape[0] - 1
    stacked = jnp.concatenate([across_ref[last], halo_ref[last]], axis=0)
    weights = grouped_ref[jnp.where(tile_ref[0] == TILES - 1, 1, 0), (GROUP - 1) * 16 :]
    out_ref[...] = dot(weights, stacked).astype(jnp.bfloat16)


def last_planar(tile, across, halo, grouped):
    return pl.pallas_call(
        last_kernel,
        in_specs=[whole(pltpu.SMEM)] + [whole()] * 3,
        out_specs=whole(),
        out_shape=jax.ShapeDtypeStruct((16, HALF), jnp.bfloat16),
        compiler_params=params(),
        name="last_planar",
    )(tile, across, halo, grouped)


def blend(before, middle, after):
    total = before.astype(jnp.float32) + 2.0 * middle.astype(jnp.float32)
    return ((total + after.astype(jnp.float32)) * 0.25).astype(jnp.bfloat16)


def section_kernel(
    tile_ref, across_ref, halo_ref, grouped_ref, table_ref, out_ref, head_ref, planar_ref
):
    groups = across_ref.shape[0]
    weights = grouped_ref[jnp.where(tile_ref[0] == TILES - 1, 1, 0)]
    for g in range(groups):
        stacked = jnp.concatenate([across_ref[g], halo_ref[g]], axis=0)
        planar = dot(weights, stacked).astype(jnp.bfloat16)
        planar_ref[g * GROUP : (g + 1) * GROUP] = planar.reshape(GROUP, 16, HALF)
    head_ref[0] = planar_ref[0]
    head_ref[16] = planar_ref[1]
    table = table_ref[...]
    sections = groups * GROUP // 2
    for m in range(sections // 16):
        made = [
            blend(planar_ref[2 * s - 1], planar_ref[2 * s], planar_ref[2 * s + 1])
            for s in range(max(1, m * 16), (m + 1) * 16)
        ]
        if m == 0:
            for k in range(15):
                head_ref[1 + k] = made[k]
            continue
        rows = jnp.concatenate(made, axis=0)
        out_ref[:, m * HALF : (m + 1) * HALF] = dot_nt(table, rows).astype(jnp.bfloat16)


def row_spectra(tile, across, halo, grouped, table):
    planes = across.shape[0] * GROUP
    rows = planes // 2 * 16
    return pl.pallas_call(
        section_kernel,
        in_specs=[whole(pltpu.SMEM)] + [whole()] * 4,
        out_specs=[whole()] * 2,
        out_shape=[
            jax.ShapeDtypeStruct((HALF, rows), jnp.bfloat16),
            jax.ShapeDtypeStruct((17, 16, HALF), jnp.bfloat16),
        ],
        scratch_shapes=[pltpu.VMEM((planes, 16, HALF), jnp.bfloat16)],
        compiler_params=params(),
        cost_estimate=pl.CostEstimate(
            flops=2 * planes * 16 * 288 * HALF,
            bytes_accessed=planes * 32 * HALF * 2,
            transcendentals=0,
        ),
        name="row_spectra",
    )(tile, across, halo, grouped, table)


def head_kernel(
    tile_ref, slab_ref, next_ref, behind_ref, corner_ref, blur_ref, single_ref,
    head_ref, table_ref, spectra_ref, out_ref,
):
    rows = jnp.concatenate([behind_ref[...], corner_ref[:8]], axis=0)
    rows = dot(rows, blur_ref[...]).astype(jnp.bfloat16)
    weights = single_ref[jnp.where(tile_ref[0] == TILES - 1, 1, 0)]
    far = dot(weights, rows)
    wrapped = lax.rem(slab_ref[0], DEPTH) == 0
    before = jnp.where(wrapped, far, next_ref[...].astype(jnp.float32))
    first = blend(before.astype(jnp.bfloat16), head_ref[0], head_ref[16])
    rows = jnp.concatenate([first] + [head_ref[k] for k in range(1, 16)], axis=0)
    out_ref[...] = dot_nt(table_ref[...], rows).astype(jnp.bfloat16)


def head_spectra(tile, slab, near, behind, corner, blur, single, head, table, spectra):
    return pl.pallas_call(
        head_kernel,
        grid=(1,),
        in_specs=[whole(pltpu.SMEM)] * 2 + [whole()] * 7 + [pl.BlockSpec(memory_space=pl.ANY)],
        out_specs=pl.BlockSpec((HALF, HALF), lambda g: (0, 0)),
        out_shape=jax.ShapeDtypeStruct(spectra.shape, jnp.bfloat16),
        input_output_aliases={9: 0},
        compiler_params=params(),
        name="head_spectra",
    )(tile, slab, near, behind, corner, blur, single, head, table, spectra)


def cross_kernel(
    tile_ref, meta_ref, spectra_ref, table_ref, out_ref, held_ref, band_ref
):
    pairs = meta_ref.shape[1]
    blocks = spectra_ref.shape[2] // 128
    lane = lax.broadcasted_iota(jnp.int32, (16, 128), 1)
    out_ref[...] = jnp.zeros_like(out_ref)
    for k in range(blocks):
        for h in range(2):
            a = [
                spectra_ref[8 * h + t, :, 128 * k : 128 * (k + 1)].astype(jnp.float32)
                for t in range(8)
            ]
            for bit in (1, 2, 4):
                low = (lane // 16) & bit == 0
                for i in range(8):
                    if i & bit:
                        continue
                    j = i + bit
                    first = jnp.where(low, a[i], pltpu.roll(a[j], 16 * bit, 1))
                    second = jnp.where(low, pltpu.roll(a[i], 128 - 16 * bit, 1), a[j])
                    a[i], a[j] = first, second
            for s in range(8):
                held_ref[8 * k + s, h] = a[s]

    batch = 32
    steps = pairs // batch
    eight = (FREQS, 128)
    column = lax.broadcasted_iota(jnp.int32, eight, 1)
    special = (lax.broadcasted_iota(jnp.int32, eight, 0) == 0) & (tile_ref[0] == 0)
    upper = column > BAND // 2

    def cut(step, buffer):
        for p in range(batch):
            n = step * batch + p
            live = lane < meta_ref[4, n]
            for side in range(2):
                which = meta_ref[side, n]
                start = meta_ref[2 + side, n]
                from_low = (lane >= start) & (lane < start + 128)
                mixed = jnp.where(from_low, held_ref[which, 0], held_ref[which, 1])
                turned = pltpu.roll(mixed, (256 - start) & 127, 1)
                band = jnp.where(live, turned, 0.0)
                band_ref[buffer, 2 * p + side] = band.astype(jnp.bfloat16)

    def cross(step, buffer):
        bands = band_ref[buffer].reshape(2 * batch * 16, 128)
        full = dot(bands, table_ref[...])
        for p in range(batch):
            real, imag, edge_real, edge_imag = [], [], [], []
            for side in range(2):
                at = (2 * p + side) * 16
                cos_re = full[at : at + 8, :128]
                sin_re = full[at : at + 8, 128:]
                cos_im = full[at + 8 : at + 16, :128]
                sin_im = full[at + 8 : at + 16, 128:]
                real.append(cos_re + jnp.where(special, 0.0, sin_im))
                imag.append(jnp.where(special, 0.0, cos_im) - sin_re)
                edge_real.append(cos_im)
                edge_imag.append(-sin_im)
            cross_real = real[0] * real[1] + imag[0] * imag[1]
            cross_imag = imag[0] * real[1] - real[0] * imag[1]
            last_real = edge_real[0] * edge_real[1] + edge_imag[0] * edge_imag[1]
            last_imag = edge_imag[0] * edge_real[1] - edge_real[0] * edge_imag[1]
            first_slot = jnp.where(special & upper, cross_imag, cross_real)
            packed = jnp.where(upper, last_imag, last_real)
            second_slot = jnp.where(special, packed, cross_imag)
            both = jnp.concatenate([first_slot, second_slot], axis=0)
            out_ref[meta_ref[5, step * batch + p]] = both.astype(jnp.bfloat16)

    cut(0, 0)

    def body(step, _):
        cross(step, step & 1)
        cut(step + 1, (step + 1) & 1)
        return 0

    lax.fori_loop(0, steps - 1, body, 0)
    cross(steps - 1, (steps - 1) & 1)


def pair_table(sections, rows, extents, owners):
    position = jnp.arange(owners.shape[0], dtype=jnp.int32)
    earlier = (owners[:, None] == owners[None, :]) & (position[None, :] < position[:, None])
    slots = jnp.sum(earlier.astype(jnp.int32), axis=1)
    places = owners * OWN_CAP + slots
    return jnp.concatenate([sections.T, rows.T - 1, extents[None], places[None]], axis=0)


def cross_spectra(tile, meta, spectra, table):
    held = spectra.shape[2] // 16
    return pl.pallas_call(
        cross_kernel,
        in_specs=[whole(pltpu.SMEM)] * 2 + [whole()] * 2,
        out_specs=whole(),
        out_shape=jax.ShapeDtypeStruct((TILES * OWN_CAP, 16, 128), jnp.bfloat16),
        scratch_shapes=[
            pltpu.VMEM((held, 2, 16, 128), jnp.float32),
            pltpu.VMEM((2, 64, 16, 128), jnp.bfloat16),
        ],
        compiler_params=params(),
        name="cross_spectra",
    )(tile, meta, spectra, table)


def surface_kernel(
    cross_ref, reversal_ref, column_ref, row_ref, out_hbm, turned_ref, size_ref,
    norm_ref, col_ref, out_ref, sems,
):
    lane = lax.broadcasted_iota(jnp.int32, (FREQS, 128), 1)
    top = lax.broadcasted_iota(jnp.int32, (FREQS, 128), 0) == 0
    edge = lax.broadcasted_iota(jnp.int32, (128, 128), 1) == 0
    upper = lane > BAND // 2
    ends = (lane == 0) | (lane == BAND // 2)

    turned = dot(cross_ref[0].reshape(OWN_CAP * 16, 128), reversal_ref[...])
    turned_ref[...] = turned.reshape(OWN_CAP, 16, 128)

    def unpack(packed, turned):
        real = jnp.where(upper, turned, packed)
        imag = jnp.where(upper, packed, jnp.where(ends, 0.0, -turned))
        return real, imag

    def rounded(value):
        return value.astype(jnp.bfloat16).astype(jnp.float32)

    def replaced(row, rows):
        return jnp.concatenate([jnp.where(top, row, rows[:8]), rows[8:]], axis=0)

    def parts(slot):
        block = cross_ref[:, slot].astype(jnp.float32)
        real = block[:, :8, :].reshape(128, 128)
        imag = block[:, 8:, :].reshape(128, 128)
        turned = turned_ref[slot]
        real_0, imag_0 = unpack(real[:8], turned[:8])
        real_n, imag_n = unpack(imag[:8], turned[8:])
        return replaced(real_0, real), replaced(imag_0, imag), real_n, imag_n

    def magnitude(real, imag):
        power = real * real + imag * imag
        return power * lax.rsqrt(jnp.maximum(power, 1e-30))

    means = []
    for slot in range(OWN_CAP):
        real, imag, real_n, imag_n = parts(slot)
        size = magnitude(real, imag)
        size_n = magnitude(real_n, imag_n)
        size_ref[slot, :128] = size
        size_ref[slot, 128:] = size_n
        total = 2.0 * jnp.sum(size.reshape(16, 8, 128), axis=0)
        total = jnp.sum(total + jnp.where(top, size_n - size[:8], 0.0))
        means.append(total / (BAND * HALF) + 1e-06)
    for slot in range(OWN_CAP):
        real, imag, real_n, imag_n = parts(slot)
        scale = 1.0 / (size_ref[slot, :128] + means[slot])
        scale_n = 1.0 / (size_ref[slot, 128:] + means[slot])
        norm_real = real * scale
        norm_imag = imag * scale
        zero = rounded(norm_real[:8]) - rounded(norm_imag[:8])
        last = rounded(real_n * scale_n) - rounded(imag_n * scale_n)
        norm_ref[slot, :128] = replaced(zero, norm_real).astype(jnp.bfloat16)
        norm_ref[slot, 128:] = replaced(last, norm_imag).astype(jnp.bfloat16)
    for slot in range(OWN_CAP):
        full = dot_nt(column_ref[...], norm_ref[slot])
        cos_re, cos_im = full[:128, :128], full[:128, 128:]
        sin_re, sin_im = full[128:, :128], full[128:, 128:]
        col_real = cos_re + jnp.where(edge, sin_re, -sin_im)
        col_imag = cos_im + jnp.where(edge, sin_im, sin_re)
        col_ref[slot, :, :128] = col_real.astype(jnp.bfloat16)
        col_ref[slot, :, 128:] = col_imag.astype(jnp.bfloat16)
    step = 3
    copies = []
    for k in range(OWN_CAP // step):
        held = slice(k * step, (k + 1) * step)
        made = dot(col_ref[held].reshape(step * BAND, HALF), row_ref[...])
        out_ref[held] = made.astype(jnp.bfloat16).reshape(step, BAND, HALF)
        held = pl.ds(k * step, step)
        copies.append(
            pltpu.make_async_copy(out_ref.at[held], out_hbm.at[held], sems.at[k])
        )
        copies[-1].start()
    for copy in copies:
        copy.wait()


def surfaces(cross, back, column, row):
    return pl.pallas_call(
        surface_kernel,
        in_specs=[whole()] * 4,
        out_specs=whole(pltpu.HBM),
        out_shape=jax.ShapeDtypeStruct((OWN_CAP, BAND, HALF), jnp.bfloat16),
        scratch_shapes=[
            pltpu.VMEM((OWN_CAP, 16, 128), jnp.float32),
            pltpu.VMEM((OWN_CAP, 136, 128), jnp.float32),
            pltpu.VMEM((OWN_CAP, HALF, 128), jnp.bfloat16),
            pltpu.VMEM((OWN_CAP, BAND, HALF), jnp.bfloat16),
            pltpu.VMEM((OWN_CAP, BAND, HALF), jnp.bfloat16),
            pltpu.SemaphoreType.DMA((4,)),
        ],
        compiler_params=params(),
        name="surfaces",
    )(cross, back, column, row)


def correlate(raw_planes, pair_sections, pair_rows, pair_extent, pair_owner):
    tile = lax.axis_index("tile").astype(jnp.int32).reshape(1)
    slab = lax.axis_index("plane").astype(jnp.int32).reshape(1)
    slabs = lax.axis_size("plane")
    owners = pair_owner[:, 0]

    far = [s for s in range(slabs - 1) if (s + 1) % DEPTH == 0]
    near = [s for s in range(slabs - 1) if (s + 1) % DEPTH]
    turns = [((t + 1) % TILES, t) for t in range(TILES)]
    corners = [(s * TILES + t, (s + 1) * TILES + u) for s in far for t, u in turns]
    table = pltpu.with_memory_space_constraint(jnp.asarray(blur_matrix()), pltpu.HBM)
    held = pltpu.with_memory_space_constraint(raw_planes, pltpu.HBM)
    edges = blur_edges(held, table)
    last = raw_planes[raw_planes.shape[0] - 1]
    halo = lax.ppermute(edges, "tile", turns)
    behind = lax.ppermute(last, "plane", [(s, s + 1) for s in far])
    corner = lax.ppermute(last, ("plane", "tile"), corners)
    across = blur_across(raw_planes, blur_matrix())
    grouped, single = column_tables()
    meta = pair_table(pair_sections, pair_rows, pair_extent, owners)
    last = last_planar(tile, across, halo, grouped)
    last = lax.ppermute(last, "plane", [(s, s + 1) for s in near])
    spectra, head = row_spectra(tile, across, halo, grouped, row_transform_table())
    spectra = head_spectra(
        tile, slab, last, behind, corner, blur_matrix(), single, head,
        row_transform_table(), spectra,
    )
    spectra, meta = lax.optimization_barrier((spectra, meta))
    spectra = lax.all_to_all(
        spectra.reshape(TILES, 16, spectra.shape[1]), "tile", 0, 0, tiled=True
    )

    cos_band, sin_band = dft_tables(BAND)
    cross = cross_spectra(
        tile, meta, spectra, np.concatenate([cos_band, sin_band], axis=1)
    )
    cross = lax.all_to_all(
        cross.reshape(TILES, OWN_CAP * 16, 128), "tile", 0, 0, tiled=True
    )
    return surfaces(
        cross.reshape(TILES, OWN_CAP, 16, 128),
        reversal(),
        np.concatenate([cos_band, sin_band], axis=0),
        row_inverse_table(),
    )


def solution(mesh):
    return jax.shard_map(
        correlate,
        mesh=mesh,
        in_specs=(
            P("plane", "tile", None),
            P("plane", None),
            P("plane", None),
            P("plane"),
            P("plane", None),
        ),
        out_specs=P(("plane", "tile"), None, None),
        check_vma=False,
    )
```

```python
import math

import jax
import jax.numpy as jnp
import numpy as np
from jax import lax
from jax.experimental import pallas as pl
from jax.experimental.pallas import tpu as pltpu
from jax.sharding import PartitionSpec as P

BAND = 128
OWN_CAP = 12
FACE = 512
HALF = 256
TILES = 16
DEPTH = 8
HALO = 3
FREQS = 8
GROUP = 8
VMEM_LIMIT = 24 * 1024 * 1024


def whole(space=pltpu.VMEM):
    return pl.BlockSpec(memory_space=space)


def params(**kw):
    return pltpu.CompilerParams(vmem_limit_bytes=VMEM_LIMIT, **kw)


def blur_weight(offset):
    offset = abs(offset)
    return (6.0, 4.0, 1.0)[offset] / 16.0 if offset <= 2 else 0.0


def blur_matrix():
    table = np.zeros((FACE, HALF), np.float32)
    for c in range(FACE):
        for j in range(HALF):
            if abs(c - 2 * j) <= 2:
                table[c, j] = blur_weight(c - 2 * j)
    return table.astype(jnp.bfloat16)


def dft_tables(length):
    indices = np.arange(length)
    phases = indices[:, None] * indices[None, :] % length
    angles = phases.astype(np.float32) * np.float32(2.0 * math.pi / length)
    factor = np.float32(1.0 / math.sqrt(length))
    return (
        (np.cos(angles) * factor).astype(jnp.bfloat16),
        (np.sin(angles) * factor).astype(jnp.bfloat16),
    )


def column_weights(last_tile):
    local = np.zeros((16, 32), np.float32)
    halo = np.zeros((16, HALO), np.float32)
    for i in range(16):
        for c in range(32):
            local[i, c] = blur_weight(c - 2 - 2 * i)
        for h in range(HALO):
            halo[i, h] = blur_weight(30 + h - 2 * i)
    if last_tile:
        halo[14, :] = 0.0
        local[15, :] = 0.0
    return local, halo


def column_tables():
    width = 32 + HALO
    grouped = np.zeros((2, GROUP * 16, GROUP * width), np.float32)
    single = np.zeros((2, 16, 40), np.float32)
    for variant in (0, 1):
        local, halo = column_weights(variant == 1)
        for q in range(GROUP):
            rows = slice(q * 16, q * 16 + 16)
            grouped[variant, rows, q * 32 : q * 32 + 32] = local
            at = GROUP * 32 + q * HALO
            grouped[variant, rows, at : at + HALO] = halo
        single[variant, :, :32] = local
        single[variant, :, 32 : 32 + HALO] = halo
    return grouped.astype(jnp.bfloat16), single.astype(jnp.bfloat16)


def row_transform_table():
    cos_half, sin_half = dft_tables(HALF)
    table = np.zeros((HALF, HALF), np.float32)
    for d in range(TILES):
        for f in range(FREQS):
            v = d * FREQS + f
            table[d * 16 + f] = cos_half[v]
            if v:
                table[d * 16 + FREQS + f] = -sin_half[v].astype(np.float32)
            else:
                table[d * 16 + FREQS + f] = cos_half[HALF // 2]
    return table.astype(jnp.bfloat16)


def row_inverse_table():
    cos_half, sin_half = dft_tables(HALF)
    table = np.zeros((HALF, HALF), np.float32)
    for v in range(HALF // 2):
        table[v] = cos_half[v].astype(np.float32) * (2.0 if v else 1.0)
        if v:
            table[HALF // 2 + v] = sin_half[v].astype(np.float32) * -2.0
        else:
            table[HALF // 2] = cos_half[HALF // 2]
    return table.astype(jnp.bfloat16)


def reversal():
    table = np.zeros((BAND, BAND), np.float32)
    for u in range(BAND):
        table[(BAND - u) % BAND, u] = 1.0
    return table.astype(jnp.bfloat16)


def dot(a, b):
    return jnp.dot(a, b, preferred_element_type=jnp.float32)


def dot_nt(a, b):
    return lax.dot_general(
        a, b, (((1,), (1,)), ((), ())), preferred_element_type=jnp.float32
    )


def plane_kernel(raw_ref, table_hbm, last_ref, across_ref, edge_ref, table_ref, sems):
    planes = raw_ref.shape[0]
    table_copy = pltpu.make_async_copy(table_hbm, table_ref, sems.at[0])
    plane_copy = pltpu.make_async_copy(raw_ref.at[planes - 1], last_ref, sems.at[1])
    table_copy.start()
    plane_copy.start()
    table_copy.wait()
    plane_copy.wait()
    across = dot(last_ref[...], table_ref[...]).astype(jnp.bfloat16)
    across_ref[...] = across
    edge_ref[...] = across[:8]


def blur_last(raw, table):
    return pl.pallas_call(
        plane_kernel,
        in_specs=[whole(pltpu.HBM)] * 2,
        out_specs=[whole()] * 3,
        out_shape=[
            jax.ShapeDtypeStruct((32, FACE), jnp.bfloat16),
            jax.ShapeDtypeStruct((32, HALF), jnp.bfloat16),
            jax.ShapeDtypeStruct((8, HALF), jnp.bfloat16),
        ],
        scratch_shapes=[
            pltpu.VMEM((FACE, HALF), jnp.bfloat16),
            pltpu.SemaphoreType.DMA((2,)),
        ],
        compiler_params=params(),
        name="blur_last",
    )(raw, table)


def across_kernel(raw_ref, table_ref, across_ref, edge_ref):
    planes = raw_ref.shape[0]
    part = 16
    per = part // GROUP
    shape = (GROUP * HALO, GROUP * 8)
    row = lax.broadcasted_iota(jnp.int32, shape, 0)
    source = lax.broadcasted_iota(jnp.int32, shape, 1)
    wanted = (source >> 3) * HALO + (source & 7)
    select = jnp.where((row == wanted) & ((source & 7) < HALO), 1.0, 0.0)
    select = select.astype(jnp.bfloat16)
    for k in range(planes // part):
        cells = raw_ref[k * part : (k + 1) * part].reshape(part * 32, FACE)
        across = dot(cells, table_ref[...])
        held = across.astype(jnp.bfloat16).reshape(per, GROUP * 32, HALF)
        across_ref[k * per : (k + 1) * per] = held
        for g in range(per):
            at = g * GROUP * 32
            tops = [across[at + 32 * q : at + 32 * q + 8] for q in range(GROUP)]
            tops = jnp.concatenate(tops, axis=0).astype(jnp.bfloat16)
            edge_ref[k * per + g] = dot(select, tops).astype(jnp.bfloat16)


def blur_across(raw, table):
    planes = raw.shape[0]
    groups = planes // GROUP
    return pl.pallas_call(
        across_kernel,
        in_specs=[whole()] * 2,
        out_specs=[whole()] * 2,
        out_shape=[
            jax.ShapeDtypeStruct((groups, GROUP * 32, HALF), jnp.bfloat16),
            jax.ShapeDtypeStruct((groups, GROUP * HALO, HALF), jnp.bfloat16),
        ],
        compiler_params=params(),
        cost_estimate=pl.CostEstimate(
            flops=2 * planes * 32 * FACE * HALF,
            bytes_accessed=planes * 32 * (FACE + HALF) * 2,
            transcendentals=0,
        ),
        name="blur_across",
    )(raw, table)


def last_kernel(tile_ref, across_ref, halo_ref, single_ref, out_ref):
    rows = jnp.concatenate([across_ref[...], halo_ref[...]], axis=0)
    weights = single_ref[jnp.where(tile_ref[0] == TILES - 1, 1, 0)]
    out_ref[...] = dot(weights, rows).astype(jnp.bfloat16)


def last_planar(tile, across, halo, single):
    return pl.pallas_call(
        last_kernel,
        in_specs=[whole(pltpu.SMEM)] + [whole()] * 3,
        out_specs=whole(),
        out_shape=jax.ShapeDtypeStruct((16, HALF), jnp.bfloat16),
        compiler_params=params(),
        name="last_planar",
    )(tile, across, halo, single)


def blend(before, middle, after):
    total = before.astype(jnp.float32) + 2.0 * middle.astype(jnp.float32)
    return ((total + after.astype(jnp.float32)) * 0.25).astype(jnp.bfloat16)


def section_kernel(
    tile_ref, across_ref, halo_ref, grouped_ref, table_ref, out_ref, head_ref, planar_ref
):
    groups = across_ref.shape[0]
    weights = grouped_ref[jnp.where(tile_ref[0] == TILES - 1, 1, 0)]
    for g in range(groups):
        stacked = jnp.concatenate([across_ref[g], halo_ref[g]], axis=0)
        planar = dot(weights, stacked).astype(jnp.bfloat16)
        planar_ref[g * GROUP : (g + 1) * GROUP] = planar.reshape(GROUP, 16, HALF)
    head_ref[0] = planar_ref[0]
    head_ref[16] = planar_ref[1]
    table = table_ref[...]
    sections = groups * GROUP // 2
    for m in range(sections // 16):
        made = [
            blend(planar_ref[2 * s - 1], planar_ref[2 * s], planar_ref[2 * s + 1])
            for s in range(max(1, m * 16), (m + 1) * 16)
        ]
        if m == 0:
            for k in range(15):
                head_ref[1 + k] = made[k]
            continue
        rows = jnp.concatenate(made, axis=0)
        out_ref[:, m * HALF : (m + 1) * HALF] = dot_nt(table, rows).astype(jnp.bfloat16)


def row_spectra(tile, across, halo, grouped, table):
    planes = across.shape[0] * GROUP
    rows = planes // 2 * 16
    return pl.pallas_call(
        section_kernel,
        in_specs=[whole(pltpu.SMEM)] + [whole()] * 4,
        out_specs=[whole()] * 2,
        out_shape=[
            jax.ShapeDtypeStruct((HALF, rows), jnp.bfloat16),
            jax.ShapeDtypeStruct((17, 16, HALF), jnp.bfloat16),
        ],
        scratch_shapes=[pltpu.VMEM((planes, 16, HALF), jnp.bfloat16)],
        compiler_params=params(),
        cost_estimate=pl.CostEstimate(
            flops=2 * planes * 16 * 288 * HALF,
            bytes_accessed=planes * 32 * HALF * 2,
            transcendentals=0,
        ),
        name="row_spectra",
    )(tile, across, halo, grouped, table)


def head_kernel(
    tile_ref, slab_ref, next_ref, behind_ref, corner_ref, blur_ref, single_ref,
    head_ref, table_ref, spectra_ref, out_ref,
):
    rows = jnp.concatenate([behind_ref[...], corner_ref[:8]], axis=0)
    rows = dot(rows, blur_ref[...]).astype(jnp.bfloat16)
    weights = single_ref[jnp.where(tile_ref[0] == TILES - 1, 1, 0)]
    far = dot(weights, rows)
    wrapped = lax.rem(slab_ref[0], DEPTH) == 0
    before = jnp.where(wrapped, far, next_ref[...].astype(jnp.float32))
    first = blend(before.astype(jnp.bfloat16), head_ref[0], head_ref[16])
    rows = jnp.concatenate([first] + [head_ref[k] for k in range(1, 16)], axis=0)
    out_ref[...] = dot_nt(table_ref[...], rows).astype(jnp.bfloat16)


def head_spectra(tile, slab, near, behind, corner, blur, single, head, table, spectra):
    return pl.pallas_call(
        head_kernel,
        grid=(1,),
        in_specs=[whole(pltpu.SMEM)] * 2 + [whole()] * 7 + [pl.BlockSpec(memory_space=pl.ANY)],
        out_specs=pl.BlockSpec((HALF, HALF), lambda g: (0, 0)),
        out_shape=jax.ShapeDtypeStruct(spectra.shape, jnp.bfloat16),
        input_output_aliases={9: 0},
        compiler_params=params(),
        name="head_spectra",
    )(tile, slab, near, behind, corner, blur, single, head, table, spectra)


def cross_kernel(
    tile_ref, meta_ref, spectra_ref, table_ref, out_ref, held_ref, band_ref
):
    pairs = meta_ref.shape[1]
    blocks = spectra_ref.shape[2] // 128
    lane = lax.broadcasted_iota(jnp.int32, (16, 128), 1)
    out_ref[...] = jnp.zeros_like(out_ref)
    for k in range(blocks):
        for h in range(2):
            a = [
                spectra_ref[8 * h + t, :, 128 * k : 128 * (k + 1)].astype(jnp.float32)
                for t in range(8)
            ]
            for bit in (1, 2, 4):
                low = (lane // 16) & bit == 0
                for i in range(8):
                    if i & bit:
                        continue
                    j = i + bit
                    first = jnp.where(low, a[i], pltpu.roll(a[j], 16 * bit, 1))
                    second = jnp.where(low, pltpu.roll(a[i], 128 - 16 * bit, 1), a[j])
                    a[i], a[j] = first, second
            for s in range(8):
                held_ref[8 * k + s, h] = a[s]

    batch = 32
    steps = pairs // batch
    eight = (FREQS, 128)
    column = lax.broadcasted_iota(jnp.int32, eight, 1)
    special = (lax.broadcasted_iota(jnp.int32, eight, 0) == 0) & (tile_ref[0] == 0)
    upper = column > BAND // 2

    def cut(step, buffer):
        for p in range(batch):
            n = step * batch + p
            live = lane < meta_ref[4, n]
            for side in range(2):
                which = meta_ref[side, n]
                start = meta_ref[2 + side, n]
                from_low = (lane >= start) & (lane < start + 128)
                mixed = jnp.where(from_low, held_ref[which, 0], held_ref[which, 1])
                turned = pltpu.roll(mixed, (256 - start) & 127, 1)
                band = jnp.where(live, turned, 0.0)
                band_ref[buffer, 2 * p + side] = band.astype(jnp.bfloat16)

    def cross(step, buffer):
        bands = band_ref[buffer].reshape(2 * batch * 16, 128)
        full = dot(bands, table_ref[...])
        for p in range(batch):
            real, imag, edge_real, edge_imag = [], [], [], []
            for side in range(2):
                at = (2 * p + side) * 16
                cos_re = full[at : at + 8, :128]
                sin_re = full[at : at + 8, 128:]
                cos_im = full[at + 8 : at + 16, :128]
                sin_im = full[at + 8 : at + 16, 128:]
                real.append(cos_re + jnp.where(special, 0.0, sin_im))
                imag.append(jnp.where(special, 0.0, cos_im) - sin_re)
                edge_real.append(cos_im)
                edge_imag.append(-sin_im)
            cross_real = real[0] * real[1] + imag[0] * imag[1]
            cross_imag = imag[0] * real[1] - real[0] * imag[1]
            last_real = edge_real[0] * edge_real[1] + edge_imag[0] * edge_imag[1]
            last_imag = edge_imag[0] * edge_real[1] - edge_real[0] * edge_imag[1]
            first_slot = jnp.where(special & upper, cross_imag, cross_real)
            packed = jnp.where(upper, last_imag, last_real)
            second_slot = jnp.where(special, packed, cross_imag)
            both = jnp.concatenate([first_slot, second_slot], axis=0)
            out_ref[meta_ref[5, step * batch + p]] = both.astype(jnp.bfloat16)

    cut(0, 0)

    def body(step, _):
        cross(step, step & 1)
        cut(step + 1, (step + 1) & 1)
        return 0

    lax.fori_loop(0, steps - 1, body, 0)
    cross(steps - 1, (steps - 1) & 1)


def pair_table(sections, rows, extents, owners):
    position = jnp.arange(owners.shape[0], dtype=jnp.int32)
    earlier = (owners[:, None] == owners[None, :]) & (position[None, :] < position[:, None])
    slots = jnp.sum(earlier.astype(jnp.int32), axis=1)
    places = owners * OWN_CAP + slots
    return jnp.concatenate([sections.T, rows.T - 1, extents[None], places[None]], axis=0)


def cross_spectra(tile, meta, spectra, table):
    held = spectra.shape[2] // 16
    return pl.pallas_call(
        cross_kernel,
        in_specs=[whole(pltpu.SMEM)] * 2 + [whole()] * 2,
        out_specs=whole(),
        out_shape=jax.ShapeDtypeStruct((TILES * OWN_CAP, 16, 128), jnp.bfloat16),
        scratch_shapes=[
            pltpu.VMEM((held, 2, 16, 128), jnp.float32),
            pltpu.VMEM((2, 64, 16, 128), jnp.bfloat16),
        ],
        compiler_params=params(),
        name="cross_spectra",
    )(tile, meta, spectra, table)


def surface_kernel(
    cross_ref, reversal_ref, column_ref, row_ref, out_hbm, turned_ref, size_ref,
    norm_ref, col_ref, out_ref, sems,
):
    lane = lax.broadcasted_iota(jnp.int32, (FREQS, 128), 1)
    top = lax.broadcasted_iota(jnp.int32, (FREQS, 128), 0) == 0
    edge = lax.broadcasted_iota(jnp.int32, (128, 128), 1) == 0
    upper = lane > BAND // 2
    ends = (lane == 0) | (lane == BAND // 2)

    turned = dot(cross_ref[0].reshape(OWN_CAP * 16, 128), reversal_ref[...])
    turned_ref[...] = turned.reshape(OWN_CAP, 16, 128)

    def unpack(packed, turned):
        real = jnp.where(upper, turned, packed)
        imag = jnp.where(upper, packed, jnp.where(ends, 0.0, -turned))
        return real, imag

    def rounded(value):
        return value.astype(jnp.bfloat16).astype(jnp.float32)

    def replaced(row, rows):
        return jnp.concatenate([jnp.where(top, row, rows[:8]), rows[8:]], axis=0)

    def parts(slot):
        block = cross_ref[:, slot].astype(jnp.float32)
        real = block[:, :8, :].reshape(128, 128)
        imag = block[:, 8:, :].reshape(128, 128)
        turned = turned_ref[slot]
        real_0, imag_0 = unpack(real[:8], turned[:8])
        real_n, imag_n = unpack(imag[:8], turned[8:])
        return replaced(real_0, real), replaced(imag_0, imag), real_n, imag_n

    def magnitude(real, imag):
        power = real * real + imag * imag
        return power * lax.rsqrt(jnp.maximum(power, 1e-30))

    means = []
    for slot in range(OWN_CAP):
        real, imag, real_n, imag_n = parts(slot)
        size = magnitude(real, imag)
        size_n = magnitude(real_n, imag_n)
        size_ref[slot, :128] = size
        size_ref[slot, 128:] = size_n
        total = 2.0 * jnp.sum(size.reshape(16, 8, 128), axis=0)
        total = jnp.sum(total + jnp.where(top, size_n - size[:8], 0.0))
        means.append(total / (BAND * HALF) + 1e-06)
    for slot in range(OWN_CAP):
        real, imag, real_n, imag_n = parts(slot)
        scale = 1.0 / (size_ref[slot, :128] + means[slot])
        scale_n = 1.0 / (size_ref[slot, 128:] + means[slot])
        norm_real = real * scale
        norm_imag = imag * scale
        zero = rounded(norm_real[:8]) - rounded(norm_imag[:8])
        last = rounded(real_n * scale_n) - rounded(imag_n * scale_n)
        norm_ref[slot, :128] = replaced(zero, norm_real).astype(jnp.bfloat16)
        norm_ref[slot, 128:] = replaced(last, norm_imag).astype(jnp.bfloat16)
    for slot in range(OWN_CAP):
        full = dot_nt(column_ref[...], norm_ref[slot])
        cos_re, cos_im = full[:128, :128], full[:128, 128:]
        sin_re, sin_im = full[128:, :128], full[128:, 128:]
        col_real = cos_re + jnp.where(edge, sin_re, -sin_im)
        col_imag = cos_im + jnp.where(edge, sin_im, sin_re)
        col_ref[slot, :, :128] = col_real.astype(jnp.bfloat16)
        col_ref[slot, :, 128:] = col_imag.astype(jnp.bfloat16)
    step = 3
    copies = []
    for k in range(OWN_CAP // step):
        held = slice(k * step, (k + 1) * step)
        made = dot(col_ref[held].reshape(step * BAND, HALF), row_ref[...])
        out_ref[held] = made.astype(jnp.bfloat16).reshape(step, BAND, HALF)
        held = pl.ds(k * step, step)
        copies.append(
            pltpu.make_async_copy(out_ref.at[held], out_hbm.at[held], sems.at[k])
        )
        copies[-1].start()
    for copy in copies:
        copy.wait()


def surfaces(cross, back, column, row):
    return pl.pallas_call(
        surface_kernel,
        in_specs=[whole()] * 4,
        out_specs=whole(pltpu.HBM),
        out_shape=jax.ShapeDtypeStruct((OWN_CAP, BAND, HALF), jnp.bfloat16),
        scratch_shapes=[
            pltpu.VMEM((OWN_CAP, 16, 128), jnp.float32),
            pltpu.VMEM((OWN_CAP, 136, 128), jnp.float32),
            pltpu.VMEM((OWN_CAP, HALF, 128), jnp.bfloat16),
            pltpu.VMEM((OWN_CAP, BAND, HALF), jnp.bfloat16),
            pltpu.VMEM((OWN_CAP, BAND, HALF), jnp.bfloat16),
            pltpu.SemaphoreType.DMA((4,)),
        ],
        compiler_params=params(),
        name="surfaces",
    )(cross, back, column, row)


def correlate(raw_planes, pair_sections, pair_rows, pair_extent, pair_owner):
    tile = lax.axis_index("tile").astype(jnp.int32).reshape(1)
    slab = lax.axis_index("plane").astype(jnp.int32).reshape(1)
    slabs = lax.axis_size("plane")
    owners = pair_owner[:, 0]

    far = [s for s in range(slabs - 1) if (s + 1) % DEPTH == 0]
    near = [s for s in range(slabs - 1) if (s + 1) % DEPTH]
    turns = [((t + 1) % TILES, t) for t in range(TILES)]
    corners = [(s * TILES + t, (s + 1) * TILES + u) for s in far for t, u in turns]
    table = pltpu.with_memory_space_constraint(jnp.asarray(blur_matrix()), pltpu.HBM)
    held = pltpu.with_memory_space_constraint(raw_planes, pltpu.HBM)
    grouped, single = column_tables()
    raw_last, last, edge = blur_last(held, table)
    corner = lax.ppermute(raw_last, ("plane", "tile"), corners)
    behind = lax.ppermute(raw_last, "plane", [(s, s + 1) for s in far])
    edge = lax.ppermute(edge, "tile", turns)
    across, edges = blur_across(raw_planes, blur_matrix())
    halo = lax.ppermute(edges, "tile", turns)
    last = last_planar(tile, last, edge, single)
    last = lax.ppermute(last, "plane", [(s, s + 1) for s in near])
    meta = pair_table(pair_sections, pair_rows, pair_extent, owners)
    spectra, head = row_spectra(tile, across, halo, grouped, row_transform_table())
    spectra = head_spectra(
        tile, slab, last, behind, corner, blur_matrix(), single, head,
        row_transform_table(), spectra,
    )
    spectra, meta = lax.optimization_barrier((spectra, meta))
    spectra = lax.all_to_all(
        spectra.reshape(TILES, 16, spectra.shape[1]), "tile", 0, 0, tiled=True
    )

    cos_band, sin_band = dft_tables(BAND)
    cross = cross_spectra(
        tile, meta, spectra, np.concatenate([cos_band, sin_band], axis=1)
    )
    cross = lax.all_to_all(
        cross.reshape(TILES, OWN_CAP * 16, 128), "tile", 0, 0, tiled=True
    )
    return surfaces(
        cross.reshape(TILES, OWN_CAP, 16, 128),
        reversal(),
        np.concatenate([cos_band, sin_band], axis=0),
        row_inverse_table(),
    )


def solution(mesh):
    return jax.shard_map(
        correlate,
        mesh=mesh,
        in_specs=(
            P("plane", "tile", None),
            P("plane", None),
            P("plane", None),
            P("plane"),
            P("plane", None),
        ),
        out_specs=P(("plane", "tile"), None, None),
        check_vma=False,
    )
```
